32 devices in a mesh: blocks: 8 (over z, x), span: 4 (over y, core).
Axes of the slice: x: 2, y: 2, z: 4, core: 2. Of those that a mesh axis runs over, the one named last changes fastest.
Arguments:
- struct_disp: float32 [3, 16384], P(None, ('blocks', 'span')), may hold values from -3 to 3
- rec_struct: int32 [16384], P(('blocks', 'span')), may hold values from 0 to 511
- rec_block: int32 [16384, 1], P(('blocks', 'span')), may hold values from 0 to 7; in each aligned block of 512 rows (0 to 511, 512 to 1023, ...) at most 128 rows name the same one
- rec_node: int32 [16384], P(('blocks', 'span')), may hold values from 0 to 8191
- rec_weight: float32 [16384], P(('blocks', 'span')), may hold values from 0.2 to 1
- offset: float32 [3, 16, 256, 1024], P(None, None, 'blocks', 'span'), may hold values from -0.6 to 0.6
- prior_warp: float32 [3, 16, 256, 1024], P(None, None, 'blocks', 'span'), may hold values from -3 to 3
- inv_volume: float32 [16, 256, 1024], P(None, 'blocks', 'span'), may hold values from 0.04 to 0.16
- coord_cot: float32 [3, 16, 256, 1024], P(None, None, 'blocks', 'span'), may hold values from -6 to 6
- vol_cot: float32 [16, 256, 1024], P(None, 'blocks', 'span'), may hold values from -6 to 6
Outputs:
- warp_field: float32 [3, 16, 256, 1024], P(None, None, 'blocks', 'span')
- mesh_adjoint: float32 [3, 16, 256, 1024], P(None, None, 'blocks', 'span')
- struct_sens: float32 [3, 16384], P(None, ('blocks', 'span'))
The draws below stay inside these ranges and needn't reach their ends.
Inputs may be any that keep to these rules, and one draw needn't show every extreme that they name: `rec_block`: in the rows of one device no fluid group is named by more than 128 records, and on some devices one group is named by exactly 128.
All inputs are finite; a program needn't handle non-finite values.
Results may differ from the reference program's by a relative error of at most 0.00002.
Values sent between devices are 32-bit elements; how exact they have to be, the bound alone decides.
A program may use at most 128 MiB of HBM per device.

```python
import math
import jax
import jax.numpy as jnp
import numpy as np
from jax import lax

WALL_N = 16
CHORD_DEV = 32
SPAN_DEV = 256
SWEEPS = 4
CAPACITY = 128
SNODE_DEV = 512
GROUPS = 8
SLABS = 4
REC_DEV = 512
RECORDS = 16384
SNODES = 16384
CHORD = 256
SPANW = 1024
SURF_DEV = 8192


def with_ends(result, stream_key, smallest, top_value):
    place = [jax.random.randint(jax.random.fold_in(stream_key, axis), (), 0, length) for axis, length in enumerate(result.shape)]
    main_axis = result.shape.index(max(result.shape))
    beside = place[:main_axis] + [(place[main_axis] + 1) % result.shape[main_axis]] + place[main_axis + 1:]
    return result.at[tuple(place)].set(smallest).at[tuple(beside)].set(top_value)


def steps_of(stream_key, dims, split, smallest, high):
    level = 1.0
    for axis_at, blocks in split:
        draws = jax.random.uniform(jax.random.fold_in(jax.random.fold_in(stream_key, 6), axis_at), (blocks,), jnp.float32, smallest / len(split), high / len(split))
        level = level * jnp.repeat(jnp.exp(draws), dims[axis_at] // blocks).reshape((-1,) + (1,) * (len(dims) - 1 - axis_at))
    return level


def assign_block(stream_key, own, number, rows, count, top, bound, skew):
    sequence = jax.random.permutation(stream_key, count)
    heavy_load, ordinary = load_shares(count, rows * top, bound, skew, True), load_shares(count, rows * top, bound, skew, False)
    places = jnp.arange(count)

    def named(tallies, turn):
        used = int((tallies > 0).sum())
        fixed = max(1, used // 4)
        shifted = fixed + (places - fixed + turn * (used - fixed)) % max(1, count - fixed)
        return jnp.zeros((count,), jnp.int32).at[sequence[jnp.where(places < fixed, places, shifted)]].set(jnp.asarray(tallies, jnp.int32))

    tallies = jnp.where(number % 4 == 0, named(heavy_load, number // 4), named(ordinary, number - number // 4 - 1))
    mixed = jax.random.permutation(jax.random.fold_in(own, 3), count)
    donor, taker = mixed[0:count // 2 * 2:2], mixed[1:count // 2 * 2:2]
    margin = jnp.minimum(tallies[donor] - 1, bound - tallies[taker]) // 2
    margin = jnp.where((donor == sequence[0]) | (taker == sequence[0]) | (tallies[taker] == 0), 0, jnp.maximum(margin, 0))
    shifted = jax.random.randint(jax.random.fold_in(own, 4), (count // 2,), 0, 1 << 20) % (margin + 1)
    tallies = tallies.at[donor].add(-shifted).at[taker].add(shifted)
    labels = jnp.searchsorted(jnp.cumsum(tallies), jnp.arange(rows * top), side="right").astype(jnp.int32)
    grid = labels.reshape(top, rows).T
    grid = grid[jax.random.permutation(jax.random.fold_in(own, 1), rows)]
    turn = jax.random.randint(jax.random.fold_in(own, 2), (rows, 1), 0, top)
    return jnp.take_along_axis(grid, (jnp.arange(top)[None, :] + turn) % top, axis=1)


def load_shares(amount, total, most, slope, full):
    weights = [(1 << 20) // math.isqrt(standing ** slope) + 1 for standing in range(1, amount + 1)]
    largest = most if full else min(most, max(-(-total // amount), total * weights[0] // sum(weights)))
    least = 1 if total - largest >= amount - 1 else 0
    given, rest = [largest] + [least] * (amount - 1), total - largest - least * (amount - 1)
    while rest > 0:
        movable = [i for i in range(1, amount) if given[i] < largest] or [i for i in range(1, amount) if given[i] < most]
        whole, remaining = sum([weights[i] for i in movable]), rest
        for i in movable:
            more = min(most - given[i], max(1, remaining * weights[i] // whole), rest)
            given[i] = given[i] + more
            rest = rest - more
    return np.array(given)


def noise(rng, dims, width, most, pieces=(), held_as=jnp.bfloat16):
    entries = jax.random.normal(rng, dims, jnp.float32) * width
    if len(pieces) > 0:
        entries = steps_of(rng, dims, pieces, -0.22, 0.18) * entries
    return jnp.clip(entries, min=-most, max=most).astype(held_as)


def setup_inputs(seed: int = 0) -> dict:
    key_list = jax.random.split(jax.random.key(seed), 11)
    struct_disp = noise(key_list[0], (3, SNODES), 0.5, 3.0, ((1, 32),), jnp.float32)
    rec_struct = with_ends(jax.random.randint(key_list[1], (RECORDS,), 0, SNODE_DEV), jax.random.fold_in(key_list[1], 1), 0, SNODE_DEV - 1).astype(jnp.int32)
    rec_block_keys = jax.random.split(jax.random.fold_in(key_list[2], 1), RECORDS // REC_DEV)
    rec_block_turns = jax.random.permutation(jax.random.fold_in(key_list[2], 3), RECORDS // REC_DEV)
    rec_block = jax.vmap(lambda own, number: assign_block(jax.random.fold_in(key_list[2], 2), own, number, REC_DEV, GROUPS, 1, CAPACITY, 2))(rec_block_keys, rec_block_turns).reshape((RECORDS, 1))
    rec_node = with_ends(jax.random.randint(key_list[3], (RECORDS,), 0, SURF_DEV), jax.random.fold_in(key_list[3], 1), 0, SURF_DEV - 1).astype(jnp.int32)
    rec_weight = jnp.clip(0.2 + 0.8 * jax.random.uniform(key_list[4], (RECORDS,), jnp.float32) ** steps_of(key_list[4], (RECORDS,), ((0, 32),), -0.2, 0.2), 0.2, 1.0)
    offset = noise(key_list[5], (3, WALL_N, CHORD, SPANW), 0.1, 0.6, ((2, 8), (3, 4)), jnp.float32)
    prior_warp = noise(key_list[6], (3, WALL_N, CHORD, SPANW), 0.5, 3.0, ((2, 8), (3, 4)), jnp.float32)
    inv_volume = jnp.clip(jnp.exp(math.log(0.16) - 1.3862944 * jax.random.uniform(key_list[7], (WALL_N, CHORD, SPANW), jnp.float32) ** steps_of(key_list[7], (WALL_N, CHORD, SPANW), ((1, 8), (2, 4)), -0.2, 0.2)), 0.04, 0.16)
    coord_cot = noise(key_list[8], (3, WALL_N, CHORD, SPANW), 1.0, 6.0, ((2, 8), (3, 4)), jnp.float32)
    vol_cot = noise(key_list[9], (WALL_N, CHORD, SPANW), 1.0, 6.0, ((1, 8), (2, 4)), jnp.float32)
    return {"struct_disp": struct_disp, "rec_struct": rec_struct, "rec_block": rec_block, "rec_node": rec_node, "rec_weight": rec_weight, "offset": offset, "prior_warp": prior_warp, "inv_volume": inv_volume, "coord_cot": coord_cot, "vol_cot": vol_cot}


def neighbours(field):
    padded = jnp.pad(field, ((0, 0), (1, 1), (1, 1), (1, 1)))
    summed = padded[:, 1:-1, 2:, 1:-1] + padded[:, 1:-1, :-2, 1:-1] + padded[:, 1:-1, 1:-1, 2:] + padded[:, 1:-1, 1:-1, :-2]
    return summed + padded[:, 2:, 1:-1, 1:-1] + padded[:, :-2, 1:-1, 1:-1]


def cross_of(left, right):
    return jnp.stack([left[1] * right[2] - left[2] * right[1], left[2] * right[0] - left[0] * right[2], left[0] * right[1] - left[1] * right[0]])


def add_unit(field, axis_number):
    return field + jnp.eye(3, dtype=jnp.float32)[axis_number][:, None, None, None]


def lower_of(field, dim_number):
    widths = [(0, 0)] * field.ndim
    widths[dim_number] = (1, 0)
    padded = jnp.pad(field, widths)
    return lax.slice_in_dim(padded, 0, field.shape[dim_number], axis=dim_number)


def reference(struct_disp, rec_struct, rec_block, rec_node, rec_weight, offset, prior_warp, inv_volume, coord_cot, vol_cot):
    owner = jnp.arange(RECORDS, dtype=jnp.int32) // REC_DEV
    slab_index = owner % SLABS
    target = rec_block[:, 0]
    node_j = target * CHORD_DEV + rec_node // SPAN_DEV
    node_k = slab_index * SPAN_DEV + rec_node % SPAN_DEV
    struct_row = owner * SNODE_DEV + rec_struct
    moved_rows = struct_disp[:, struct_row] * rec_weight[None, :]
    surface = jnp.zeros((3, CHORD, SPANW), jnp.float32).at[:, node_j, node_k].add(moved_rows)
    wall_index = jnp.arange(WALL_N)
    interior = (wall_index > 0) & (wall_index < WALL_N - 1)
    relax = jnp.where(interior[:, None, None], inv_volume, 0.0)
    warp_field = prior_warp.at[:, 0].set(surface)
    for sweep_index in range(SWEEPS):
        warp_field = warp_field + relax * (neighbours(warp_field) - 6.0 * warp_field)
    shaped = offset + warp_field
    padded = jnp.pad(shaped, ((0, 0), (0, 0), (0, 1), (0, 1)))
    up_i = jnp.pad(shaped[:, 1:], ((0, 0), (0, 1), (0, 0), (0, 0)))
    edge_i = add_unit(up_i - shaped, 0)
    edge_j = add_unit(padded[:, :, 1:, :-1] - shaped, 1)
    edge_k = add_unit(padded[:, :, :-1, 1:] - shaped, 2)
    inside = (wall_index < WALL_N - 1)[:, None, None] & (jnp.arange(CHORD) < CHORD - 1)[None, :, None] & (jnp.arange(SPANW) < SPANW - 1)[None, None, :]
    weight_cell = jnp.where(inside, vol_cot, 0.0)
    grad_i = weight_cell * cross_of(edge_j, edge_k)
    grad_j = weight_cell * cross_of(edge_k, edge_i)
    grad_k = weight_cell * cross_of(edge_i, edge_j)
    adjoint = coord_cot - grad_i + lower_of(grad_i, 1) - grad_j + lower_of(grad_j, 2) - grad_k + lower_of(grad_k, 3)
    for sweep_index in range(SWEEPS):
        flux = relax * adjoint
        adjoint = adjoint + neighbours(flux) - 6.0 * flux
    sens_wall = adjoint[:, 0]
    struct_sens = jnp.zeros((3, SNODES), jnp.float32).at[:, struct_row].add(rec_weight[None, :] * sens_wall[:, node_j, node_k])
    return warp_field, adjoint, struct_sens
```

```python
import functools

import jax
import jax.numpy as jnp
from jax import lax
from jax.experimental import pallas as pl
from jax.experimental.pallas import tpu as pltpu
from jax.sharding import PartitionSpec as P

SWEEPS = 4
WIDE = SWEEPS + 1
LANES = 128
SUB = 8
VMEM_LIMIT = 40 * 1024 * 1024
MESH = pl.DeviceIdType.MESH


def split3(x):
    hi = x.astype(jnp.bfloat16)
    rest = x - hi.astype(jnp.float32)
    mid = rest.astype(jnp.bfloat16)
    low = (rest - mid.astype(jnp.float32)).astype(jnp.bfloat16)
    return hi, mid, low


def iota(shape, dim):
    return lax.broadcasted_iota(jnp.int32, shape, dim)


def rows_plan(ni):
    inv = 3 * (ni - 1) * WIDE
    second = -(-(inv + (ni - 2) * SWEEPS) // SUB) * SUB
    total = second + -(-4 * ni // SUB) * SUB
    return inv, second, total


def columns(chunks, width):
    return -(-chunks // (LANES // width))


def kernel(
    groups,
    slabs,
    struct_h,
    block_h,
    node_h,
    weight_h,
    disp_h,
    offset_h,
    prior_h,
    inv_h,
    cot_h,
    vol_h,
    warp,
    adj,
    sens_o,
    v0,
    v1,
    v2,
    v3,
    inv,
    sb,
    low_i,
    low_j,
    rec_send,
    rec_got,
    reply_send,
    reply_got,
    ja_send,
    ja_got,
    ka_send,
    ka_got,
    surf_got,
    jc_send,
    jc_got,
    kc_send,
    kc_got,
    struct_of,
    block_of,
    node_of,
    weight_of,
    disp,
    sem_small,
    sem_rec,
    sem_reply,
    sem_halo,
    sem_in,
):
    ni, nj, nk = offset_h.shape[1:]
    tiles = nk // LANES
    every = tiles + 1
    own = slice(SUB, SUB + nj)
    top, end = slice(0, SUB), slice(SUB + nj, SUB + nj + SUB)
    all_rows = nj + 2 * SUB
    lanes_of = lambda t: slice(t * LANES, (t + 1) * LANES)
    records = struct_of.shape[0]
    f32, bf16 = jnp.float32, jnp.bfloat16
    me = lax.axis_index("blocks")
    my = lax.axis_index("span")
    zero = lax.div(me, groups)
    near = (me > 0, me < groups - 1, my > 0, my < slabs - 1)
    has = near + tuple(near[a] & near[2 + b] for a in (0, 1) for b in (0, 1))
    step_of = ((-1, 0), (1, 0), (0, -1), (0, 1), (-1, -1), (-1, 1), (1, -1), (1, 1))
    where_to = tuple((me + a, my + b) for a, b in step_of)
    back = (1, 0, 3, 2, 7, 6, 5, 4)

    def at(r, count=SUB):
        if r % SUB == 0:
            return slice(r, r + count)
        return pl.ds(zero + r, count)

    def load(number, src, dst):
        copies = []
        for t in range(tiles):
            copies.append(
                pltpu.make_async_copy(src(lanes_of(t)), dst(t), sem_in.at[number, t])
            )
            copies[-1].start()
        return copies

    small = [
        pltpu.make_async_copy(src, dst, sem_small.at[n])
        for n, (src, dst) in enumerate(
            (
                (struct_h, struct_of),
                (disp_h, disp),
                (weight_h, weight_of),
                (block_h, block_of),
                (node_h, node_of),
            )
        )
    ]
    for copy in small:
        copy.start()
    load_prior = load(0, lambda x: prior_h.at[:, :, :, x], lambda t: v0.at[:, :, t, own, :])
    load_inv = load(1, lambda x: inv_h.at[:, :, x], lambda t: inv.at[:, t, own, :])
    load_offset = load(2, lambda x: offset_h.at[:, :, :, x], lambda t: sb.at[0:3, :, t, own, :])
    load_vol = load(3, lambda x: vol_h.at[:, :, x], lambda t: sb.at[3, :, t, own, :])
    load_cot = load(4, lambda x: cot_h.at[:, :, :, x], lambda t: adj.at[:, :, t, own, :])

    def arrived(copies):
        for copy in copies:
            copy.wait()

    barrier = pltpu.get_barrier_semaphore()
    greeted = groups - 1
    for d in range(2, 8):
        greeted = greeted + has[d].astype(jnp.int32)

        @pl.when(has[d])
        def _(d=d):
            pl.semaphore_signal(barrier, inc=1, device_id=where_to[d], device_id_type=MESH)

    for step in range(1, groups):
        pl.semaphore_signal(
            barrier, inc=1, device_id=(lax.rem(me + step, groups), my), device_id_type=MESH
        )

    def flat(ref):
        return ref[...].reshape(1, records)

    arrived(small)
    weights = flat(weight_of)
    onehot_s = (iota((disp.shape[1], records), 0) == flat(struct_of)).astype(bf16)
    parts = jnp.concatenate(split3(disp[...]), axis=0)
    gathered = jnp.dot(parts, onehot_s, preferred_element_type=f32)
    rec_send[0:3, :] = (gathered[0:3] + gathered[3:6] + gathered[6:9]) * weights
    rec_send[3:4, :] = (flat(block_of) * (nj * nk) + flat(node_of)).astype(f32)

    lane = iota((SUB, LANES), 1)
    first_lane, last_lane, left_half = lane == 0, lane == LANES - 1, lane < LANES // 2
    tile_rows = [SUB + r * SUB for r in range(nj // SUB)]

    def pack_lanes(sources, send, column, width):
        per = LANES // width
        chunk = lane // width
        chunk_last = lax.rem(lane + width, LANES) // width
        for g in range(columns(len(sources), width)):
            first = [jnp.zeros((SUB, LANES), f32) for _ in tile_rows]
            last = list(first)
            for p, source in enumerate(sources[g * per : (g + 1) * per]):
                for n, r in enumerate(tile_rows):
                    both = jnp.where(left_half, source(0, r), source(tiles - 1, r))
                    if p:
                        both = pltpu.roll(both, p * width, 1)
                    first[n] = jnp.where(chunk == p, both, first[n])
                    last[n] = jnp.where(chunk_last == p, both, last[n])
            for n in range(len(tile_rows)):
                rows = slice(n * SUB, (n + 1) * SUB)
                send[0, column + g, rows, :] = first[n]
                send[1, column + g, rows, :] = last[n]

    def unpack_lanes(targets, got, column, width, rows):
        per = LANES // width
        chunk = lane // width
        for g in range(columns(len(targets), width)):
            after = [got[0, column + g, r : r + SUB, :] for r in rows]
            before = [got[1, column + g, r : r + SUB, :] for r in rows]
            for p, target in enumerate(targets[g * per : (g + 1) * per]):
                for n, r in enumerate(rows):
                    both = jnp.where(chunk == p, after[n], before[n])
                    if p:
                        both = pltpu.roll(both, LANES - p * width, 1)
                    target(r, both)

    def edge(ref, *index):
        return lambda t, r: ref[(*index, t, slice(r, r + SUB), slice(None))]

    def halo(ref, *index):
        def put(r, value):
            ref[(*index, tiles, slice(r, r + SUB), slice(None))] = value

        return put

    inv_at, second, total_rows = rows_plan(ni)
    field_layers = [(c, i) for c in range(3) for i in range(1, ni)]
    inner = range(1, ni - 1)
    shape_layers = [(c, i) for c in range(4) for i in range(ni)]
    near_columns = columns(len(field_layers) + len(inner), WIDE)

    def take_from(s, count):
        return SUB if s == 0 else SUB + nj - count

    def put_to(s, count):
        return SUB + nj if s == 0 else SUB - count

    def pack_rows(ref, index, send, start, count, first, stop, unroll):
        @pl.loop(first, stop, unroll=unroll)
        def _(i):
            for c, source in enumerate(ref):
                for s in (0, 1):
                    for t in range(tiles):
                        spot = pl.ds(start + (c * (stop - first) + i - first) * count, count)
                        send[s, t, spot, :] = source[(*index, i, t, at(take_from(s, count), count))]

    def unpack_rows(ref, got, start, count, first, stop, unroll):
        @pl.loop(first, stop, unroll=unroll)
        def _(i):
            for c, target in enumerate(ref):
                for s in (0, 1):
                    for t in range(tiles):
                        spot = pl.ds(start + (c * (stop - first) + i - first) * count, count)
                        target[i, t, at(put_to(s, count), count)] = got[s, t, spot, :]

    level = [v0, v1, v2, v3, warp]
    field = [level[0].at[c] for c in range(3)]
    shape = [sb.at[c] for c in range(4)]

    arrived(load_prior)
    arrived(load_inv)
    pack_rows(field, (), ja_send, 0, WIDE, 1, ni, 3)
    pack_rows([inv], (), ja_send, inv_at, SWEEPS, 1, ni - 1, 2)
    pack_lanes(
        [edge(v0, c, i) for c, i in field_layers] + [edge(inv, i) for i in inner],
        ka_send,
        0,
        WIDE,
    )
    arrived(load_offset)
    arrived(load_vol)
    pack_rows(shape, (), ja_send, second, 1, 0, ni, 2)
    pack_lanes([edge(sb, c, i) for c, i in shape_layers], ka_send, near_columns, 1)

    def move(d, src, dst, number):
        return pltpu.make_async_remote_copy(
            src_ref=src,
            dst_ref=dst,
            send_sem=sem_halo.at[0, number, d],
            recv_sem=sem_halo.at[1, number, d],
            device_id=where_to[d],
            device_id_type=MESH,
        )

    def start(d, *message):
        @pl.when(has[d])
        def _():
            move(d, *message).start()

    def received(d, *message):
        @pl.when(has[back[d]])
        def _():
            move(d, *message).wait_recv()

    def sent(d, *message):
        @pl.when(has[d])
        def _():
            move(d, *message).wait_send()

    def clear_missing(d, ref):
        @pl.when(jnp.logical_not(has[back[d]]))
        def _():
            ref[...] = jnp.zeros(ref.shape, f32)

    def row_message(d, send, got, rows, number):
        return (d, send.at[d, :, rows, :], got.at[d, :, rows, :], number)

    def lane_messages(send, got, number):
        out = []
        for s in (0, 1):
            out.append((2 + s, send.at[s], got.at[s, :, own, :], number))
        for a, rows, to in ((0, slice(0, SUB), end), (1, slice(nj - SUB, nj), top)):
            for s in (0, 1):
                out.append(
                    (4 + 2 * a + s, send.at[s, :, rows, :], got.at[s, :, to, :], number)
                )
        return out

    wide_rows = [row_message(d, ja_send, ja_got, slice(0, second), 0) for d in (0, 1)]
    thin_rows = [row_message(d, ja_send, ja_got, slice(second, total_rows), 1) for d in (0, 1)]
    lanes_a = lane_messages(ka_send, ka_got, 0)
    surf = [(2 + s, v0.at[:, 0, s * (tiles - 1)], surf_got.at[s], 2) for s in (0, 1)]
    rows_c = [row_message(d, jc_send, jc_got, slice(None), 3) for d in (0, 1)]
    lanes_c = lane_messages(kc_send, kc_got, 3)
    for d, _, dst, _ in wide_rows + thin_rows + lanes_a + surf + rows_c + lanes_c:
        clear_missing(d, dst)

    def rec_copy(step):
        return pltpu.make_async_remote_copy(
            src_ref=rec_send,
            dst_ref=rec_got.at[me],
            send_sem=sem_rec.at[0, step],
            recv_sem=sem_rec.at[1, step],
            device_id=(lax.rem(me + step, groups), my),
            device_id_type=MESH,
        )

    pl.semaphore_wait(barrier, greeted)
    for message in lanes_a + wide_rows:
        start(*message)
    for step in range(1, groups):
        rec_copy(step).start()
    for message in thin_rows:
        start(*message)
    rec_got[me] = rec_send[...]

    def in_pairs(first, stop):
        def run(step):
            even = first + (stop - first) // 2 * 2
            if even > first:
                pl.loop(first, even, unroll=2)(step)
            if even < stop:
                step(even)

        return run

    def changes(src, c, i, r, count):
        x = [src[c, i, t, at(r), :] for t in range(every)]
        right = [pltpu.roll(a, 1, 1) for a in x]
        left = [pltpu.roll(a, LANES - 1, 1) for a in x]
        out = []
        for t in range(count):
            total = jnp.where(first_lane, right[t - 1], right[t])
            total = total + jnp.where(last_lane, left[(t + 1) % every], left[t])
            total = total + (src[c, i, t, at(r - 1), :] + src[c, i, t, at(r + 1), :])
            total = total + (src[c, i - 1, t, at(r), :] + src[c, i + 1, t, at(r), :])
            out.append(total - 6.0 * x[t])
        return x, out

    def sweep_a(s, first, stop, rows):
        src, dst = level[s], level[s + 1]

        @in_pairs(first, stop)
        def _(i):
            for c in range(3):
                for r in rows:
                    x, change = changes(src, c, i, r, every)
                    for t in range(every):
                        dst[c, i, t, at(r), :] = x[t] + inv[i, t, at(r), :] * change[t]

    def keep_layer(i, rows):
        for c in range(3):
            value = level[0][c, i, :, rows, :]
            for s in range(1, SWEEPS + 1):
                level[s][c, i, :, rows, :] = value

    low_row, high_row = SUB - SWEEPS, SUB + nj - SWEEPS
    outer_rows = (low_row, high_row)
    shifted_rows = list(range(low_row, high_row + 1, SUB))
    field_halos = [halo(v0, c, i) for c, i in field_layers] + [halo(inv, i) for i in inner]
    shape_halos = [halo(sb, c, i) for c, i in shape_layers]

    for message in lanes_a[:2]:
        received(*message)
    unpack_lanes(field_halos, ka_got, 0, WIDE, tile_rows)
    keep_layer(ni - 1, own)
    for s in range(SWEEPS):
        sweep_a(s, s + 2, ni - 1, tile_rows)

    row_of = (me * nj + iota((all_rows, records), 0) - SUB).astype(f32)
    col_of = iota((nk, records), 0).astype(f32)

    def target_of(code):
        row = jnp.floor((code + 0.5) * (1.0 / nk))
        return row, code - row * nk

    def scatter(g, total):
        got = rec_got[g]
        row, col = target_of(got[3:4, :])
        here = row_of == row
        cols = (col_of == col).astype(bf16)
        pieces = split3(got[0:3, :])
        left = jnp.concatenate(
            [
                jnp.where(here, pieces[n][c : c + 1, :].astype(f32), 0.0)
                for n in range(3)
                for c in range(3)
            ],
            axis=0,
        ).astype(bf16)
        out = lax.dot_general(
            left, cols, (((1,), (1,)), ((), ())), preferred_element_type=f32
        )
        rows = 3 * all_rows
        return total + (out[0:rows] + out[rows : 2 * rows] + out[2 * rows :])

    def scatter_next(step, total):
        rec_copy(step).wait_recv()
        return scatter(lax.rem(me - step + groups, groups), total)

    surface = scatter(me, jnp.zeros((3 * all_rows, nk), f32))
    surface = lax.fori_loop(1, groups, scatter_next, surface)
    for c in range(3):
        for t in range(tiles):
            v0[c, 0, t] = surface[c * all_rows : (c + 1) * all_rows, lanes_of(t)]
    for message in surf:
        start(*message)

    for message in wide_rows + lanes_a[2:]:
        received(*message)
    unpack_rows(field, ja_got, 0, WIDE, 1, ni, 3)
    unpack_rows([inv], ja_got, inv_at, SWEEPS, 1, ni - 1, 2)
    unpack_lanes(field_halos, ka_got, 0, WIDE, (0, SUB + nj))
    for rows in (top, end):
        keep_layer(ni - 1, rows)
    for s in range(SWEEPS):
        sweep_a(s, s + 2, ni - 1, outer_rows)

    for message in surf:
        received(*message)
    for c in range(3):
        for r in range(0, all_rows, SUB):
            rows = slice(r, r + SUB)
            v0[c, 0, tiles, rows, :] = jnp.where(
                left_half, surf_got[0, c, rows, :], surf_got[1, c, rows, :]
            )
    keep_layer(0, slice(0, all_rows))
    for s in range(SWEEPS):
        sweep_a(s, 1, s + 2, shifted_rows)

    for message in thin_rows:
        received(*message)
    unpack_rows(shape, ja_got, second, 1, 0, ni, 2)
    unpack_lanes(shape_halos, ka_got, near_columns, 1, range(0, all_rows, SUB))

    for r in shifted_rows:
        row_at = me * nj + iota((SUB, LANES), 0) + (r - SUB)
        row_in = (row_at >= 0) & (row_at < groups * nj - 1)
        for t in range(every):
            col_at = my * nk + lane + (t * LANES if t < tiles else -LANES)
            cell = row_in & (col_at >= 0) & (col_at < slabs * nk - 1)

            @pl.loop(0, ni, unroll=4)
            def _(i, r=r, t=t, cell=cell):
                for c in range(3):
                    sb[c, i, t, at(r), :] = sb[c, i, t, at(r), :] + warp[c, i, t, at(r), :]
                keep = cell & (i < ni - 1)
                sb[3, i, t, at(r), :] = jnp.where(keep, sb[3, i, t, at(r), :], 0.0)

    def cross(a, b):
        return (
            a[1] * b[2] - a[2] * b[1],
            a[2] * b[0] - a[0] * b[2],
            a[0] * b[1] - a[1] * b[0],
        )

    low_i[...] = jnp.zeros(low_i.shape, f32)
    arrived(load_cot)
    for message in surf:
        sent(*message)

    @pl.loop(0, ni)
    def _(i):
        above = jnp.minimum(i + 1, ni - 1)
        for r in [0] + tile_rows:
            held = None
            order = range(tiles) if r == 0 else (tiles, *range(tiles))
            for t in order:
                base = [sb[c, i, t, at(r), :] for c in range(3)]
                edge_i = [sb[c, above, t, at(r), :] - base[c] for c in range(3)]
                edge_i[0] = edge_i[0] + 1.0
                weight = sb[3, i, t, at(r), :]
                weighted_i = [weight * e for e in edge_i]
                if r > 0:
                    edge_j = [sb[c, i, t, at(r + 1), :] - base[c] for c in range(3)]
                    edge_j[1] = edge_j[1] + 1.0
                    grad_k = cross(weighted_i, edge_j)
                    moved_k = [pltpu.roll(g, 1, 1) for g in grad_k]
                if t < tiles:
                    follow = (t + 1) % every
                    edge_k = [
                        jnp.where(
                            last_lane,
                            pltpu.roll(sb[c, i, follow, at(r), :], LANES - 1, 1),
                            pltpu.roll(base[c], LANES - 1, 1),
                        )
                        - base[c]
                        for c in range(3)
                    ]
                    edge_k[2] = edge_k[2] + 1.0
                    grad_j = cross(edge_k, weighted_i)
                    for c in range(3):
                        low_j[c, t, at(r), :] = grad_j[c]
                if r > 0 and t < tiles:
                    grad_i = cross([weight * e for e in edge_j], edge_k)
                    rate = jnp.where((i > 0) & (i < ni - 1), inv[i, t, at(r), :], 0.0)
                    for c in range(3):
                        lower_k = jnp.where(first_lane, held[c], moved_k[c])
                        out = adj[c, i, t, at(r), :] - grad_i[c] + low_i[c, t, at(r), :]
                        out = out + (low_j[c, t, at(r - 1), :] - grad_j[c])
                        out = out + (lower_k - grad_k[c])
                        low_i[c, t, at(r), :] = grad_i[c]
                        adj[c, i, t, at(r), :] = out
                        v0[c, i, t, at(r), :] = rate * out
                if r > 0:
                    held = moved_k

    flux_layers = [(c, i) for c in range(3) for i in inner]
    pack_rows(field, (), jc_send, 0, SWEEPS, 1, ni - 1, 2)
    for message in rows_c:
        start(*message)
    pack_lanes([edge(v0, c, i) for c, i in flux_layers], kc_send, 0, SWEEPS)
    for message in lanes_c:
        start(*message)
    for s in range(SWEEPS):
        for c in range(3):
            for i in (0, ni - 1):
                level[s][c, i] = jnp.zeros(v0.shape[2:], f32)

    def sweep_c(s, first, stop, rows, adds):
        src = level[s]
        last = s == SWEEPS - 1

        @in_pairs(first, stop)
        def _(i):
            for c in range(3):
                for r, (low, high) in zip(rows, adds):
                    x, change = changes(src, c, i, r, tiles if last else every)
                    for t, delta in enumerate(change):
                        if t < tiles:
                            to = at(r + low, high - low)
                            adj[c, i, t, to, :] = adj[c, i, t, to, :] + delta[low:high]
                        if not last:
                            level[s + 1][c, i, t, at(r), :] = (
                                x[t] + inv[i, t, at(r), :] * delta
                            )

    whole = (0, SUB)
    flux_halos = [halo(v0, c, i) for c, i in flux_layers]
    for message in lanes_c[:2]:
        received(*message)
    unpack_lanes(flux_halos, kc_got, 0, SWEEPS, tile_rows)
    inner_adds = [whole] * len(tile_rows)
    inner_adds[0] = (SWEEPS, SUB)
    inner_adds[-1] = (0, SUB - SWEEPS)
    for s in range(SWEEPS - 1):
        sweep_c(s, 1, ni - 1, tile_rows, inner_adds)
    mid_rows = shifted_rows[1:-1]
    sweep_c(SWEEPS - 1, 1, ni - 1, mid_rows, [whole] * len(mid_rows))

    for message in rows_c + lanes_c[2:]:
        received(*message)
    unpack_rows(field, jc_got, 0, SWEEPS, 1, ni - 1, 2)
    unpack_lanes(flux_halos, kc_got, 0, SWEEPS, (0, SUB + nj))
    for s in range(SWEEPS - 1):
        sweep_c(s, 1, SWEEPS - s, outer_rows, [whole] * 2)

    def add_wall(wall, layer):
        for c in range(3):
            for t in range(tiles):
                for r in tile_rows:
                    value = adj[c, wall, t, at(r), :]
                    for s in range(SWEEPS):
                        value = value + level[s][c, layer, t, at(r), :]
                    adj[c, wall, t, at(r), :] = value

    add_wall(0, 1)

    def wall_of(c):
        return jnp.concatenate([adj[c, 0, t, own, :] for t in range(tiles)], axis=1)

    wall = jnp.concatenate(
        [jnp.concatenate(split3(wall_of(c)), axis=0) for c in range(3)], axis=0
    )
    row_w = (me * nj + iota((nj, records), 0)).astype(f32)

    def reply_copy(step):
        to = lax.rem(me + step, groups)
        return pltpu.make_async_remote_copy(
            src_ref=reply_send.at[to],
            dst_ref=reply_got.at[me],
            send_sem=sem_reply.at[0, step],
            recv_sem=sem_reply.at[1, step],
            device_id=(to, my),
            device_id_type=MESH,
        )

    def answer(g):
        row, col = target_of(rec_got[g, 3:4, :])
        cols = (col_of == col).astype(bf16)
        here = row_w == row
        out = jnp.dot(wall, cols, preferred_element_type=f32)
        for c in range(3):
            first = 3 * c * nj
            value = (
                out[first : first + nj]
                + out[first + nj : first + 2 * nj]
                + out[first + 2 * nj : first + 3 * nj]
            )
            reply_send[g, c : c + 1, :] = jnp.sum(
                jnp.where(here, value, 0.0), axis=0, keepdims=True
            )
        reply_send[g, 3:4, :] = jnp.zeros((1, records), f32)

    @pl.loop(1, groups)
    def _(step):
        answer(lax.rem(me + step, groups))
        reply_copy(step).start()

    answer(me)
    reply_got[me] = reply_send[me]

    for s in range(SWEEPS - 1):
        sweep_c(s, SWEEPS - s, ni - 1, outer_rows, [whole] * 2)
    sweep_c(SWEEPS - 1, 1, ni - 1, outer_rows, [whole] * 2)
    add_wall(ni - 1, ni - 2)

    for step in range(1, groups):
        reply_copy(step).wait_recv()
    total = lax.fori_loop(
        0, groups, lambda g, kept: kept + reply_got[g], jnp.zeros((4, records), f32)
    )
    weighted = jnp.concatenate(split3(total[0:3] * weights), axis=0)
    out = lax.dot_general(
        weighted, onehot_s, (((1,), (1,)), ((), ())), preferred_element_type=f32
    )
    sens_o[...] = out[0:3] + out[3:6] + out[6:9]
    for message in wide_rows + thin_rows + lanes_a + rows_c + lanes_c:
        sent(*message)
    for step in range(1, groups):
        reply_copy(step).wait_send()
        rec_copy(step).wait_send()


def deliver(warp, adj, sens, warp_h, adj_h, sens_h, sem):
    nj, nk = warp_h.shape[2:]
    own = slice(SUB, SUB + nj)
    copies = []
    for t in range(nk // LANES):
        lanes = slice(t * LANES, (t + 1) * LANES)
        for n, (src, dst) in enumerate(((warp, warp_h), (adj, adj_h))):
            copies.append(
                pltpu.make_async_copy(
                    src.at[:, :, t, own, :], dst.at[:, :, :, lanes], sem.at[n, t]
                )
            )
    for copy in copies:
        copy.start()
    sens_h[...] = sens[...]
    for copy in copies:
        copy.wait()


def body(
    struct_disp,
    rec_struct,
    rec_block,
    rec_node,
    rec_weight,
    offset,
    prior_warp,
    inv_volume,
    coord_cot,
    vol_cot,
):
    groups = lax.axis_size("blocks")
    slabs = lax.axis_size("span")
    _, ni, nj, nk = offset.shape
    records = rec_struct.shape[0]
    f32 = jnp.float32
    all_rows = nj + 2 * SUB
    tiles = nk // LANES
    _, _, total_rows = rows_plan(ni)
    cols_a = columns(3 * (ni - 1) + ni - 2, WIDE) + columns(4 * ni, 1)
    cols_c = columns(3 * (ni - 2), SWEEPS)
    rows_c = -(-3 * (ni - 2) * SWEEPS // SUB) * SUB

    def lane_buffers(count):
        return [
            pltpu.VMEM((2, count, nj, LANES), f32),
            pltpu.VMEM((2, count, all_rows, LANES), f32),
        ]

    vmem = pl.BlockSpec(memory_space=pltpu.VMEM)
    hbm = pl.BlockSpec(memory_space=pltpu.HBM)
    in_place = lambda x: pltpu.with_memory_space_constraint(x, pltpu.HBM)
    warp, adj, sens = pl.pallas_call(
        functools.partial(kernel, groups, slabs),
        out_shape=(
            pltpu.VMEM((3, ni, tiles + 1, all_rows, LANES), f32),
            pltpu.VMEM((3, ni, tiles, all_rows, LANES), f32),
            pltpu.VMEM(struct_disp.shape, f32),
        ),
        in_specs=[hbm] * 10,
        out_specs=[vmem] * 3,
        scratch_shapes=[
            *([pltpu.VMEM((3, ni, tiles + 1, all_rows, LANES), f32)] * SWEEPS),
            pltpu.VMEM((ni, tiles + 1, all_rows, LANES), f32),
            pltpu.VMEM((4, ni, tiles + 1, all_rows, LANES), f32),
            pltpu.VMEM((3, tiles, nj + SUB, LANES), f32),
            pltpu.VMEM((3, tiles, nj + SUB, LANES), f32),
            pltpu.VMEM((4, records), f32),
            pltpu.VMEM((groups, 4, records), f32),
            pltpu.VMEM((groups, 4, records), f32),
            pltpu.VMEM((groups, 4, records), f32),
            *([pltpu.VMEM((2, tiles, total_rows, LANES), f32)] * 2),
            *lane_buffers(cols_a),
            pltpu.VMEM((2, 3, all_rows, LANES), f32),
            *([pltpu.VMEM((2, tiles, rows_c, LANES), f32)] * 2),
            *lane_buffers(cols_c),
            *([pltpu.VMEM((records,), jnp.int32)] * 3),
            pltpu.VMEM((records,), f32),
            pltpu.VMEM(struct_disp.shape, f32),
            pltpu.SemaphoreType.DMA((5,)),
            pltpu.SemaphoreType.DMA((2, groups)),
            pltpu.SemaphoreType.DMA((2, groups)),
            pltpu.SemaphoreType.DMA((2, 4, 8)),
            pltpu.SemaphoreType.DMA((5, tiles)),
        ],
        compiler_params=pltpu.CompilerParams(
            collective_id=0, has_side_effects=True, vmem_limit_bytes=VMEM_LIMIT
        ),
        name="warp_adjoint",
    )(
        *map(
            in_place,
            (
                rec_struct,
                rec_block.reshape(records),
                rec_node,
                rec_weight,
                struct_disp,
                offset,
                prior_warp,
                inv_volume,
                coord_cot,
                vol_cot,
            ),
        )
    )
    return pl.pallas_call(
        deliver,
        out_shape=(
            jax.ShapeDtypeStruct(offset.shape, f32),
            jax.ShapeDtypeStruct(offset.shape, f32),
            jax.ShapeDtypeStruct(struct_disp.shape, f32),
        ),
        in_specs=[vmem] * 3,
        out_specs=[hbm, hbm, vmem],
        scratch_shapes=[pltpu.SemaphoreType.DMA((2, tiles))],
        compiler_params=pltpu.CompilerParams(vmem_limit_bytes=4 * 1024 * 1024),
        name="deliver",
    )(warp, adj, sens)


def solution(mesh):
    placed = (
        P(None, ("blocks", "span")),
        P(("blocks", "span")),
        P(("blocks", "span"), None),
        P(("blocks", "span")),
        P(("blocks", "span")),
        P(None, None, "blocks", "span"),
        P(None, None, "blocks", "span"),
        P(None, "blocks", "span"),
        P(None, None, "blocks", "span"),
        P(None, "blocks", "span"),
    )
    return jax.shard_map(
        body,
        mesh=mesh,
        in_specs=placed,
        out_specs=(
            P(None, None, "blocks", "span"),
            P(None, None, "blocks", "span"),
            P(None, ("blocks", "span")),
        ),
        check_vma=False,
    )
```

```python
import functools

import jax
import jax.numpy as jnp
from jax import lax
from jax.experimental import pallas as pl
from jax.experimental.pallas import tpu as pltpu
from jax.sharding import PartitionSpec as P

SWEEPS = 4
WIDE = SWEEPS + 1
LANES = 128
SUB = 8
VMEM_LIMIT = 40 * 1024 * 1024
MESH = pl.DeviceIdType.MESH


def split3(x):
    hi = x.astype(jnp.bfloat16)
    rest = x - hi.astype(jnp.float32)
    mid = rest.astype(jnp.bfloat16)
    low = (rest - mid.astype(jnp.float32)).astype(jnp.bfloat16)
    return hi, mid, low


def iota(shape, dim):
    return lax.broadcasted_iota(jnp.int32, shape, dim)


def rows_plan(ni):
    inv = 3 * (ni - 1) * WIDE
    second = -(-(inv + (ni - 2) * SWEEPS) // SUB) * SUB
    total = second + -(-4 * ni // SUB) * SUB
    return inv, second, total


def columns(chunks, width):
    return -(-chunks // (LANES // width))


def kernel(
    groups,
    slabs,
    struct_h,
    block_h,
    node_h,
    weight_h,
    disp_h,
    offset_h,
    prior_h,
    inv_h,
    cot_h,
    vol_h,
    warp,
    adj,
    sens_o,
    v0,
    v1,
    v2,
    v3,
    inv,
    sb,
    low_i,
    low_j,
    rec_send,
    rec_got,
    reply_send,
    reply_got,
    ja_send,
    ja_got,
    ka_send,
    ka_got,
    surf_got,
    jc_send,
    jc_got,
    kc_send,
    kc_got,
    struct_of,
    block_of,
    node_of,
    weight_of,
    disp,
    sem_small,
    sem_rec,
    sem_reply,
    sem_halo,
    sem_in,
):
    ni, nj, nk = offset_h.shape[1:]
    tiles = nk // LANES
    every = tiles + 1
    own = slice(SUB, SUB + nj)
    top, end = slice(0, SUB), slice(SUB + nj, SUB + nj + SUB)
    all_rows = nj + 2 * SUB
    lanes_of = lambda t: slice(t * LANES, (t + 1) * LANES)
    records = struct_of.shape[0]
    f32, bf16 = jnp.float32, jnp.bfloat16
    me = lax.axis_index("blocks")
    my = lax.axis_index("span")
    zero = lax.div(me, groups)
    near = (me > 0, me < groups - 1, my > 0, my < slabs - 1)
    has = near + tuple(near[a] & near[2 + b] for a in (0, 1) for b in (0, 1))
    step_of = ((-1, 0), (1, 0), (0, -1), (0, 1), (-1, -1), (-1, 1), (1, -1), (1, 1))
    where_to = tuple((me + a, my + b) for a, b in step_of)
    back = (1, 0, 3, 2, 7, 6, 5, 4)

    def at(r, count=SUB):
        if r % SUB == 0:
            return slice(r, r + count)
        return pl.ds(zero + r, count)

    def arrived(copies):
        for copy in copies:
            copy.wait()

    barrier = pltpu.get_barrier_semaphore()
    greeted = groups - 1
    for d in range(2, 8):
        greeted = greeted + has[d].astype(jnp.int32)

        @pl.when(has[d])
        def _(d=d):
            pl.semaphore_signal(barrier, inc=1, device_id=where_to[d], device_id_type=MESH)

    for step in range(1, groups):
        pl.semaphore_signal(
            barrier, inc=1, device_id=(lax.rem(me + step, groups), my), device_id_type=MESH
        )

    def load(number, src, dst):
        copies = []
        for t in range(tiles):
            copies.append(
                pltpu.make_async_copy(src(lanes_of(t)), dst(t), sem_in.at[number, t])
            )
            copies[-1].start()
        return copies

    small = [
        pltpu.make_async_copy(src, dst, sem_small.at[n])
        for n, (src, dst) in enumerate(
            (
                (struct_h, struct_of),
                (disp_h, disp),
                (weight_h, weight_of),
                (block_h, block_of),
                (node_h, node_of),
            )
        )
    ]
    for copy in small:
        copy.start()
    load_prior = load(0, lambda x: prior_h.at[:, :, :, x], lambda t: v0.at[:, :, t, own, :])
    load_inv = load(1, lambda x: inv_h.at[:, :, x], lambda t: inv.at[:, t, own, :])
    load_offset = load(2, lambda x: offset_h.at[:, :, :, x], lambda t: sb.at[0:3, :, t, own, :])
    load_vol = load(3, lambda x: vol_h.at[:, :, x], lambda t: sb.at[3, :, t, own, :])
    load_cot = load(4, lambda x: cot_h.at[:, :, :, x], lambda t: adj.at[:, :, t, own, :])

    def flat(ref):
        return ref[...].reshape(1, records)

    arrived(small)
    weights = flat(weight_of)
    onehot_s = (iota((disp.shape[1], records), 0) == flat(struct_of)).astype(bf16)
    parts = jnp.concatenate(split3(disp[...]), axis=0)
    gathered = jnp.dot(parts, onehot_s, preferred_element_type=f32)
    rec_send[0:3, :] = (gathered[0:3] + gathered[3:6] + gathered[6:9]) * weights
    rec_send[3:4, :] = (flat(block_of) * (nj * nk) + flat(node_of)).astype(f32)

    lane = iota((SUB, LANES), 1)
    first_lane, last_lane, left_half = lane == 0, lane == LANES - 1, lane < LANES // 2
    tile_rows = [SUB + r * SUB for r in range(nj // SUB)]

    def pack_lanes(sources, send, column, width):
        per = LANES // width
        chunk = lane // width
        chunk_last = lax.rem(lane + width, LANES) // width
        for g in range(columns(len(sources), width)):
            first = [jnp.zeros((SUB, LANES), f32) for _ in tile_rows]
            last = list(first)
            for p, source in enumerate(sources[g * per : (g + 1) * per]):
                for n, r in enumerate(tile_rows):
                    both = jnp.where(left_half, source(0, r), source(tiles - 1, r))
                    if p:
                        both = pltpu.roll(both, p * width, 1)
                    first[n] = jnp.where(chunk == p, both, first[n])
                    last[n] = jnp.where(chunk_last == p, both, last[n])
            for n in range(len(tile_rows)):
                rows = slice(n * SUB, (n + 1) * SUB)
                send[0, column + g, rows, :] = first[n]
                send[1, column + g, rows, :] = last[n]

    def unpack_lanes(targets, got, column, width, rows):
        per = LANES // width
        chunk = lane // width
        for g in range(columns(len(targets), width)):
            after = [got[0, column + g, r : r + SUB, :] for r in rows]
            before = [got[1, column + g, r : r + SUB, :] for r in rows]
            for p, target in enumerate(targets[g * per : (g + 1) * per]):
                for n, r in enumerate(rows):
                    both = jnp.where(chunk == p, after[n], before[n])
                    if p:
                        both = pltpu.roll(both, LANES - p * width, 1)
                    target(r, both)

    def edge(ref, *index):
        return lambda t, r: ref[(*index, t, slice(r, r + SUB), slice(None))]

    def halo(ref, *index):
        def put(r, value):
            ref[(*index, tiles, slice(r, r + SUB), slice(None))] = value

        return put

    inv_at, second, total_rows = rows_plan(ni)
    field_layers = [(c, i) for c in range(3) for i in range(1, ni)]
    inner = range(1, ni - 1)
    shape_layers = [(c, i) for c in range(4) for i in range(ni)]
    near_columns = columns(len(field_layers) + len(inner), WIDE)

    def take_from(s, count):
        return SUB if s == 0 else SUB + nj - count

    def put_to(s, count):
        return SUB + nj if s == 0 else SUB - count

    def pack_rows(ref, send, start, count, first, stop, unroll, sides=(0, 1)):
        @pl.loop(first, stop, unroll=unroll)
        def _(i):
            for c, source in enumerate(ref):
                for s in sides:
                    for t in range(tiles):
                        spot = pl.ds(start + (c * (stop - first) + i - first) * count, count)
                        send[s, t, spot, :] = source[i, t, at(take_from(s, count), count)]

    def unpack_rows(ref, got, start, count, first, stop, unroll, sides=(0, 1)):
        @pl.loop(first, stop, unroll=unroll)
        def _(i):
            for c, target in enumerate(ref):
                for s in sides:
                    for t in range(tiles):
                        spot = pl.ds(start + (c * (stop - first) + i - first) * count, count)
                        target[i, t, at(put_to(s, count), count)] = got[s, t, spot, :]

    level = [v0, v1, v2, v3, warp]
    field = [level[0].at[c] for c in range(3)]
    shape = [sb.at[c] for c in range(4)]

    def move(d, src, dst, number):
        return pltpu.make_async_remote_copy(
            src_ref=src,
            dst_ref=dst,
            send_sem=sem_halo.at[0, number, d],
            recv_sem=sem_halo.at[1, number, d],
            device_id=where_to[d],
            device_id_type=MESH,
        )

    def start(d, *message):
        @pl.when(has[d])
        def _():
            move(d, *message).start()

    def received(d, *message):
        @pl.when(has[back[d]])
        def _():
            move(d, *message).wait_recv()

    def sent(d, *message):
        @pl.when(has[d])
        def _():
            move(d, *message).wait_send()

    def clear_missing(d, ref):
        @pl.when(jnp.logical_not(has[back[d]]))
        def _():
            ref[...] = jnp.zeros(ref.shape, f32)

    def row_message(d, send, got, rows, number):
        return (d, send.at[d, :, rows, :], got.at[d, :, rows, :], number)

    def lane_messages(send, got, number):
        out = []
        for s in (0, 1):
            out.append((2 + s, send.at[s], got.at[s, :, own, :], number))
        for a, rows, to in ((0, slice(0, SUB), end), (1, slice(nj - SUB, nj), top)):
            for s in (0, 1):
                out.append(
                    (4 + 2 * a + s, send.at[s, :, rows, :], got.at[s, :, to, :], number)
                )
        return out

    wide_rows = [row_message(d, ja_send, ja_got, slice(0, second), 0) for d in (0, 1)]
    thin_rows = [row_message(d, ja_send, ja_got, slice(second, total_rows), 1) for d in (0, 1)]
    lanes_a = lane_messages(ka_send, ka_got, 0)
    surf = [(2 + s, v0.at[:, 0, s * (tiles - 1)], surf_got.at[s], 2) for s in (0, 1)]
    rows_c = [row_message(d, jc_send, jc_got, slice(None), 3) for d in (0, 1)]
    lanes_c = lane_messages(kc_send, kc_got, 3)
    def rec_copy(step):
        return pltpu.make_async_remote_copy(
            src_ref=rec_send,
            dst_ref=rec_got.at[me],
            send_sem=sem_rec.at[0, step],
            recv_sem=sem_rec.at[1, step],
            device_id=(lax.rem(me + step, groups), my),
            device_id_type=MESH,
        )

    arrived(load_prior)
    pack_rows(field, ja_send, 0, WIDE, 1, ni, 3)
    arrived(load_inv)
    pack_rows([inv], ja_send, inv_at, SWEEPS, 1, ni - 1, 2)
    pl.semaphore_wait(barrier, greeted)
    for step in range(1, groups):
        rec_copy(step).start()
    start(*wide_rows[0])
    pack_lanes(
        [edge(v0, c, i) for c, i in field_layers] + [edge(inv, i) for i in inner],
        ka_send,
        0,
        WIDE,
    )
    arrived(load_offset)
    arrived(load_vol)
    pack_lanes([edge(sb, c, i) for c, i in shape_layers], ka_send, near_columns, 1)
    for message in lanes_a[:2]:
        start(*message)
    pack_rows(shape, ja_send, second, 1, 0, ni, 2)
    for message in (thin_rows[0], *lanes_a[2:4], wide_rows[1], thin_rows[1], *lanes_a[4:]):
        start(*message)
    rec_got[me] = rec_send[...]
    for d, _, dst, _ in wide_rows + thin_rows + lanes_a + surf + rows_c + lanes_c:
        clear_missing(d, dst)

    def in_pairs(first, stop):
        def run(step):
            unroll = (stop - first) // 2
            even = first + 2 * unroll
            if unroll:
                pl.loop(first, even, unroll=unroll)(step)
            if even < stop:
                step(even)

        return run

    def changes(src, c, i, r, count):
        x = [src[c, i, t, at(r), :] for t in range(every)]
        if count == tiles:
            nexts = [(x[t - 1], x[t], x[(t + 1) % every]) for t in range(tiles)]
            before = [pltpu.roll(jnp.where(last_lane, a, b), 1, 1) for a, b, _ in nexts]
            after = [
                pltpu.roll(jnp.where(first_lane, d, b), LANES - 1, 1) for _, b, d in nexts
            ]
        else:
            right = [pltpu.roll(a, 1, 1) for a in x]
            left = [pltpu.roll(a, LANES - 1, 1) for a in x]
            before = [jnp.where(first_lane, right[t - 1], right[t]) for t in range(every)]
            after = [
                jnp.where(last_lane, left[(t + 1) % every], left[t]) for t in range(every)
            ]
        out = []
        for t in range(count):
            total = before[t] + after[t]
            total = total + (src[c, i, t, at(r - 1), :] + src[c, i, t, at(r + 1), :])
            total = total + (src[c, i - 1, t, at(r), :] + src[c, i + 1, t, at(r), :])
            out.append(total - 6.0 * x[t])
        return x, out

    def sweep_a(s, first, stop, rows):
        src, dst = level[s], level[s + 1]

        @in_pairs(first, stop)
        def _(i):
            for c in range(3):
                for r in rows:
                    x, change = changes(src, c, i, r, every)
                    for t in range(every):
                        dst[c, i, t, at(r), :] = x[t] + inv[i, t, at(r), :] * change[t]

    def keep_layer(i, rows):
        for c in range(3):
            value = level[0][c, i, :, rows, :]
            for s in range(1, SWEEPS + 1):
                level[s][c, i, :, rows, :] = value

    low_row, high_row = SUB - SWEEPS, SUB + nj - SWEEPS
    outer_rows = (low_row, high_row)
    shifted_rows = list(range(low_row, high_row + 1, SUB))
    field_halos = [halo(v0, c, i) for c, i in field_layers] + [halo(inv, i) for i in inner]
    shape_halos = [halo(sb, c, i) for c, i in shape_layers]

    for message in lanes_a[:2]:
        received(*message)
    unpack_lanes(field_halos, ka_got, 0, WIDE, tile_rows)
    keep_layer(ni - 1, own)
    for s in range(SWEEPS):
        sweep_a(s, s + 2, ni - 1, tile_rows)

    def target_of(code):
        row = jnp.floor((code + 0.5) * (1.0 / nk))
        return row, code - row * nk

    together = 2 if groups % 2 == 0 and records <= 4 * LANES else 1

    def side_by_side(parts):
        return parts[0] if len(parts) == 1 else jnp.concatenate(parts, axis=1)

    row_of = (me * nj + iota((all_rows, together * records), 0) - SUB).astype(f32)
    col_of = iota((nk, together * records), 0).astype(f32)

    def scatter(members, total):
        got = side_by_side([rec_got[g] for g in members])
        row, col = target_of(got[3:4, :])
        here = row_of == row
        cols = (col_of == col).astype(bf16)
        pieces = split3(got[0:3, :])
        left = jnp.concatenate(
            [
                jnp.where(here, pieces[n][c : c + 1, :].astype(f32), 0.0)
                for n in range(3)
                for c in range(3)
            ],
            axis=0,
        ).astype(bf16)
        out = lax.dot_general(
            left, cols, (((1,), (1,)), ((), ())), preferred_element_type=f32
        )
        rows = 3 * all_rows
        return total + (out[0:rows] + out[rows : 2 * rows] + out[2 * rows :])

    def scatter_next(n, total):
        steps = [n * together + k for k in range(together)]
        for step in steps:
            rec_copy(step).wait_recv()
        return scatter([lax.rem(me - step + groups, groups) for step in steps], total)

    for step in range(1, together):
        rec_copy(step).wait_recv()
    surface = scatter(
        [lax.rem(me - step + groups, groups) for step in range(together)],
        jnp.zeros((3 * all_rows, nk), f32),
    )
    surface = lax.fori_loop(1, groups // together, scatter_next, surface)
    for c in range(3):
        for t in range(tiles):
            v0[c, 0, t] = surface[c * all_rows : (c + 1) * all_rows, lanes_of(t)]
    for message in surf:
        start(*message)

    def outer(s):
        rows = (end, top)[s]
        for message in (wide_rows[s], thin_rows[s], *lanes_a[2 + 2 * s : 4 + 2 * s]):
            received(*message)
        unpack_rows(field, ja_got, 0, WIDE, 1, ni, 3, (s,))
        unpack_rows([inv], ja_got, inv_at, SWEEPS, 1, ni - 1, 2, (s,))
        unpack_lanes(field_halos, ka_got, 0, WIDE, (rows.start,))
        unpack_rows(shape, ja_got, second, 1, 0, ni, 2, (s,))
        unpack_lanes(shape_halos, ka_got, near_columns, 1, (rows.start,))
        keep_layer(ni - 1, rows)

    def shape_rows(rows):
        for r in rows:
            row_at = me * nj + iota((SUB, LANES), 0) + (r - SUB)
            row_in = (row_at >= 0) & (row_at < groups * nj - 1)
            for t in range(every):
                col_at = my * nk + lane + (t * LANES if t < tiles else -LANES)
                cell = row_in & (col_at >= 0) & (col_at < slabs * nk - 1)

                @pl.loop(0, ni, unroll=4)
                def _(i, r=r, t=t, cell=cell):
                    for c in range(3):
                        sb[c, i, t, at(r), :] = sb[c, i, t, at(r), :] + warp[c, i, t, at(r), :]
                    keep = cell & (i < ni - 1)
                    sb[3, i, t, at(r), :] = jnp.where(keep, sb[3, i, t, at(r), :], 0.0)

    outer(0)
    for s in range(SWEEPS):
        sweep_a(s, s + 2, ni - 1, (high_row,))

    unpack_lanes(shape_halos, ka_got, near_columns, 1, tile_rows)
    for message in surf:
        received(*message)
    for c in range(3):
        for r in range(0, all_rows, SUB):
            rows = slice(r, r + SUB)
            v0[c, 0, tiles, rows, :] = jnp.where(
                left_half, surf_got[0, c, rows, :], surf_got[1, c, rows, :]
            )
    keep_layer(0, slice(0, all_rows))
    for s in range(SWEEPS):
        sweep_a(s, 1, s + 2, tile_rows + [high_row])

    def cross(a, b):
        return (
            a[1] * b[2] - a[2] * b[1],
            a[2] * b[0] - a[0] * b[2],
            a[0] * b[1] - a[1] * b[0],
        )

    low_i[...] = jnp.zeros(low_i.shape, f32)
    arrived(load_cot)

    def gradients(parts):
        @pl.loop(0, ni, unroll=2)
        def _(i):
            above = jnp.minimum(i + 1, ni - 1)
            for r, full in parts:
                order = (tiles, *range(tiles)) if full else range(tiles)
                base = [[sb[c, i, t, at(r), :] for c in range(3)] for t in range(every)]
                held = None
                for t in order:
                    edge_i = [sb[c, above, t, at(r), :] - base[t][c] for c in range(3)]
                    edge_i[0] = edge_i[0] + 1.0
                    weight = sb[3, i, t, at(r), :]
                    weighted_i = [weight * e for e in edge_i]
                    if full:
                        edge_j = [sb[c, i, t, at(r + 1), :] - base[t][c] for c in range(3)]
                        edge_j[1] = edge_j[1] + 1.0
                        grad_k = cross(weighted_i, edge_j)
                    if t < tiles:
                        follow = base[(t + 1) % every]
                        edge_k = [
                            pltpu.roll(
                                jnp.where(first_lane, follow[c], base[t][c]), LANES - 1, 1
                            )
                            - base[t][c]
                            for c in range(3)
                        ]
                        edge_k[2] = edge_k[2] + 1.0
                        grad_j = cross(edge_k, weighted_i)
                        for c in range(3):
                            low_j[c, t, at(r), :] = grad_j[c]
                    if full and t < tiles:
                        grad_i = cross([weight * e for e in edge_j], edge_k)
                        rate = jnp.where((i > 0) & (i < ni - 1), inv[i, t, at(r), :], 0.0)
                        for c in range(3):
                            lower_k = pltpu.roll(
                                jnp.where(last_lane, held[c], grad_k[c]), 1, 1
                            )
                            out = adj[c, i, t, at(r), :] - grad_i[c] + low_i[c, t, at(r), :]
                            out = out + (low_j[c, t, at(r - 1), :] - grad_j[c])
                            out = out + (lower_k - grad_k[c])
                            low_i[c, t, at(r), :] = grad_i[c]
                            adj[c, i, t, at(r), :] = out
                            v0[c, i, t, at(r), :] = rate * out
                    if full:
                        held = grad_k

    flux_layers = [(c, i) for c in range(3) for i in inner]

    def send_flux(s):
        pack_rows(field, jc_send, 0, SWEEPS, 1, ni - 1, 2, (s,))
        start(*rows_c[s])

    for message in surf:
        sent(*message)
    shape_rows(shifted_rows[1:])
    gradients([(tile_rows[0], False)] + [(r, True) for r in tile_rows[1:]])
    send_flux(1)

    outer(1)
    for s in range(SWEEPS):
        sweep_a(s, 1, ni - 1, (low_row,))
    shape_rows(shifted_rows[:1])
    gradients([(0, False), (tile_rows[0], True)])
    send_flux(0)
    pack_lanes([edge(v0, c, i) for c, i in flux_layers], kc_send, 0, SWEEPS)
    for message in lanes_c:
        start(*message)
    for s in range(SWEEPS):
        for c in range(3):
            for i in (0, ni - 1):
                level[s][c, i] = jnp.zeros(v0.shape[2:], f32)

    def sweep_c(s, first, stop, rows, adds):
        src = level[s]
        last = s == SWEEPS - 1

        @in_pairs(first, stop)
        def _(i):
            for c in range(3):
                for r, (low, high) in zip(rows, adds):
                    x, change = changes(src, c, i, r, tiles if last else every)
                    for t, delta in enumerate(change):
                        if t < tiles:
                            to = at(r + low, high - low)
                            adj[c, i, t, to, :] = adj[c, i, t, to, :] + delta[low:high]
                        if not last:
                            level[s + 1][c, i, t, at(r), :] = (
                                x[t] + inv[i, t, at(r), :] * delta
                            )

    whole = (0, SUB)
    flux_halos = [halo(v0, c, i) for c, i in flux_layers]
    for message in lanes_c[:2]:
        received(*message)
    unpack_lanes(flux_halos, kc_got, 0, SWEEPS, tile_rows)
    inner_adds = [whole] * len(tile_rows)
    inner_adds[0] = (SWEEPS, SUB)
    inner_adds[-1] = (0, SUB - SWEEPS)
    for s in range(SWEEPS - 1):
        sweep_c(s, 1, ni - 1, tile_rows, inner_adds)
    mid_rows = shifted_rows[1:-1]
    sweep_c(SWEEPS - 1, 1, ni - 1, mid_rows, [whole] * len(mid_rows))

    for message in rows_c + lanes_c[2:]:
        received(*message)
    unpack_rows(field, jc_got, 0, SWEEPS, 1, ni - 1, 2)
    unpack_lanes(flux_halos, kc_got, 0, SWEEPS, (0, SUB + nj))
    for s in range(SWEEPS - 1):
        sweep_c(s, 1, SWEEPS - s, outer_rows, [whole] * 2)

    def add_wall(wall, layer):
        for c in range(3):
            for t in range(tiles):
                for r in tile_rows:
                    value = adj[c, wall, t, at(r), :]
                    for s in range(SWEEPS):
                        value = value + level[s][c, layer, t, at(r), :]
                    adj[c, wall, t, at(r), :] = value

    add_wall(0, 1)

    def wall_of(c):
        return jnp.concatenate([adj[c, 0, t, own, :] for t in range(tiles)], axis=1)

    wall = jnp.concatenate(
        [jnp.concatenate(split3(wall_of(c)), axis=0) for c in range(3)], axis=0
    )
    row_w = (me * nj + iota((nj, together * records), 0)).astype(f32)

    def reply_copy(step):
        to = lax.rem(me + step, groups)
        return pltpu.make_async_remote_copy(
            src_ref=reply_send.at[to],
            dst_ref=reply_got.at[me],
            send_sem=sem_reply.at[0, step],
            recv_sem=sem_reply.at[1, step],
            device_id=(to, my),
            device_id_type=MESH,
        )

    def answer(members):
        row, col = target_of(side_by_side([rec_got[g, 3:4, :] for g in members]))
        cols = (col_of == col).astype(bf16)
        here = row_w == row
        out = jnp.dot(wall, cols, preferred_element_type=f32)
        for c in range(3):
            first = 3 * c * nj
            value = (
                out[first : first + nj]
                + out[first + nj : first + 2 * nj]
                + out[first + 2 * nj : first + 3 * nj]
            )
            found = jnp.sum(jnp.where(here, value, 0.0), axis=0, keepdims=True)
            for n, g in enumerate(members):
                reply_send[g, c : c + 1, :] = found[:, n * records : (n + 1) * records]
        for g in members:
            reply_send[g, 3:4, :] = jnp.zeros((1, records), f32)

    def answer_next(n, last):
        steps = [n * together + k + 1 for k in range(together)]
        answer([lax.rem(me + step, groups) for step in steps])
        for step in steps[: together - 1] if last else steps:
            reply_copy(step).start()

    @pl.loop(0, groups // together - 1)
    def _(n):
        answer_next(n, False)

    answer_next(groups // together - 1, True)
    reply_got[me] = reply_send[me]

    for s in range(SWEEPS - 1):
        sweep_c(s, SWEEPS - s, ni - 1, outer_rows, [whole] * 2)
    sweep_c(SWEEPS - 1, 1, ni - 1, outer_rows, [whole] * 2)
    add_wall(ni - 1, ni - 2)

    for step in range(1, groups):
        reply_copy(step).wait_recv()
    total = lax.fori_loop(
        0, groups, lambda g, kept: kept + reply_got[g], jnp.zeros((4, records), f32)
    )
    weighted = jnp.concatenate(split3(total[0:3] * weights), axis=0)
    out = lax.dot_general(
        weighted, onehot_s, (((1,), (1,)), ((), ())), preferred_element_type=f32
    )
    sens_o[...] = out[0:3] + out[3:6] + out[6:9]
    for message in wide_rows + thin_rows + lanes_a + rows_c + lanes_c:
        sent(*message)
    for step in range(1, groups):
        reply_copy(step).wait_send()
        rec_copy(step).wait_send()


def deliver(warp, adj, sens, warp_h, adj_h, sens_h, sem):
    nj, nk = warp_h.shape[2:]
    own = slice(SUB, SUB + nj)
    copies = []
    for n, (src, dst) in enumerate(((warp, warp_h), (adj, adj_h))):
        for c in range(3):
            for t in range(nk // LANES):
                lanes = slice(t * LANES, (t + 1) * LANES)
                copies.append(
                    pltpu.make_async_copy(
                        src.at[c, :, t, own, :], dst.at[c, :, :, lanes], sem.at[n, c, t]
                    )
                )
                copies[-1].start()
    sens_h[...] = sens[...]
    for copy in copies:
        copy.wait()


def body(
    struct_disp,
    rec_struct,
    rec_block,
    rec_node,
    rec_weight,
    offset,
    prior_warp,
    inv_volume,
    coord_cot,
    vol_cot,
):
    groups = lax.axis_size("blocks")
    slabs = lax.axis_size("span")
    _, ni, nj, nk = offset.shape
    records = rec_struct.shape[0]
    f32 = jnp.float32
    all_rows = nj + 2 * SUB
    tiles = nk // LANES
    _, _, total_rows = rows_plan(ni)
    cols_a = columns(3 * (ni - 1) + ni - 2, WIDE) + columns(4 * ni, 1)
    cols_c = columns(3 * (ni - 2), SWEEPS)
    rows_c = -(-3 * (ni - 2) * SWEEPS // SUB) * SUB

    def lane_buffers(count):
        return [
            pltpu.VMEM((2, count, nj, LANES), f32),
            pltpu.VMEM((2, count, all_rows, LANES), f32),
        ]

    vmem = pl.BlockSpec(memory_space=pltpu.VMEM)
    hbm = pl.BlockSpec(memory_space=pltpu.HBM)
    in_place = lambda x: pltpu.with_memory_space_constraint(x, pltpu.HBM)
    warp, adj, sens = pl.pallas_call(
        functools.partial(kernel, groups, slabs),
        out_shape=(
            pltpu.VMEM((3, ni, tiles + 1, all_rows, LANES), f32),
            pltpu.VMEM((3, ni, tiles, all_rows, LANES), f32),
            pltpu.VMEM(struct_disp.shape, f32),
        ),
        in_specs=[hbm] * 10,
        out_specs=[vmem] * 3,
        scratch_shapes=[
            *([pltpu.VMEM((3, ni, tiles + 1, all_rows, LANES), f32)] * SWEEPS),
            pltpu.VMEM((ni, tiles + 1, all_rows, LANES), f32),
            pltpu.VMEM((4, ni, tiles + 1, all_rows, LANES), f32),
            pltpu.VMEM((3, tiles, nj + SUB, LANES), f32),
            pltpu.VMEM((3, tiles, nj + SUB, LANES), f32),
            pltpu.VMEM((4, records), f32),
            pltpu.VMEM((groups, 4, records), f32),
            pltpu.VMEM((groups, 4, records), f32),
            pltpu.VMEM((groups, 4, records), f32),
            *([pltpu.VMEM((2, tiles, total_rows, LANES), f32)] * 2),
            *lane_buffers(cols_a),
            pltpu.VMEM((2, 3, all_rows, LANES), f32),
            *([pltpu.VMEM((2, tiles, rows_c, LANES), f32)] * 2),
            *lane_buffers(cols_c),
            *([pltpu.VMEM((records,), jnp.int32)] * 3),
            pltpu.VMEM((records,), f32),
            pltpu.VMEM(struct_disp.shape, f32),
            pltpu.SemaphoreType.DMA((5,)),
            pltpu.SemaphoreType.DMA((2, groups)),
            pltpu.SemaphoreType.DMA((2, groups)),
            pltpu.SemaphoreType.DMA((2, 4, 8)),
            pltpu.SemaphoreType.DMA((5, tiles)),
        ],
        compiler_params=pltpu.CompilerParams(
            collective_id=0, has_side_effects=True, vmem_limit_bytes=VMEM_LIMIT
        ),
        name="warp_adjoint",
    )(
        *map(
            in_place,
            (
                rec_struct,
                rec_block.reshape(records),
                rec_node,
                rec_weight,
                struct_disp,
                offset,
                prior_warp,
                inv_volume,
                coord_cot,
                vol_cot,
            ),
        )
    )
    return pl.pallas_call(
        deliver,
        out_shape=(
            jax.ShapeDtypeStruct(offset.shape, f32),
            jax.ShapeDtypeStruct(offset.shape, f32),
            jax.ShapeDtypeStruct(struct_disp.shape, f32),
        ),
        in_specs=[vmem] * 3,
        out_specs=[hbm, hbm, vmem],
        scratch_shapes=[pltpu.SemaphoreType.DMA((2, 3, tiles))],
        compiler_params=pltpu.CompilerParams(vmem_limit_bytes=4 * 1024 * 1024),
        name="deliver",
    )(warp, adj, sens)


def solution(mesh):
    placed = (
        P(None, ("blocks", "span")),
        P(("blocks", "span")),
        P(("blocks", "span"), None),
        P(("blocks", "span")),
        P(("blocks", "span")),
        P(None, None, "blocks", "span"),
        P(None, None, "blocks", "span"),
        P(None, "blocks", "span"),
        P(None, None, "blocks", "span"),
        P(None, "blocks", "span"),
    )
    return jax.shard_map(
        body,
        mesh=mesh,
        in_specs=placed,
        out_specs=(
            P(None, None, "blocks", "span"),
            P(None, None, "blocks", "span"),
            P(None, ("blocks", "span")),
        ),
        check_vma=False,
    )
```

```python
import functools

import jax
import jax.numpy as jnp
from jax import lax
from jax.experimental import pallas as pl
from jax.experimental.pallas import tpu as pltpu
from jax.sharding import PartitionSpec as P

SWEEPS = 4
WIDE = SWEEPS + 1
LANES = 128
SUB = 8
VMEM_LIMIT = 40 * 1024 * 1024
MESH = pl.DeviceIdType.MESH


def split3(x):
    hi = x.astype(jnp.bfloat16)
    rest = x - hi.astype(jnp.float32)
    mid = rest.astype(jnp.bfloat16)
    low = (rest - mid.astype(jnp.float32)).astype(jnp.bfloat16)
    return hi, mid, low


def iota(shape, dim):
    return lax.broadcasted_iota(jnp.int32, shape, dim)


def rows_plan(ni):
    inv = 3 * (ni - 1) * WIDE
    second = -(-(inv + (ni - 2) * SWEEPS) // SUB) * SUB
    total = second + -(-4 * ni // SUB) * SUB
    return inv, second, total


def columns(chunks, width):
    return -(-chunks // (LANES // width))


def kernel(
    groups,
    slabs,
    struct_h,
    block_h,
    node_h,
    weight_h,
    disp_h,
    offset_h,
    prior_h,
    inv_h,
    cot_h,
    vol_h,
    warp,
    adj,
    sens_o,
    v0,
    v1,
    v2,
    v3,
    inv,
    sb,
    low_i,
    low_j,
    rec_send,
    rec_got,
    reply_send,
    reply_got,
    ja_send,
    ja_got,
    ka_send,
    ka_got,
    surf_got,
    jc_send,
    jc_got,
    kc_send,
    kc_got,
    struct_of,
    block_of,
    node_of,
    weight_of,
    disp,
    sem_small,
    sem_rec,
    sem_reply,
    sem_halo,
    sem_in,
):
    ni, nj, nk = offset_h.shape[1:]
    tiles = nk // LANES
    every = tiles + 1
    own = slice(SUB, SUB + nj)
    top, end = slice(0, SUB), slice(SUB + nj, SUB + nj + SUB)
    all_rows = nj + 2 * SUB
    lanes_of = lambda t: slice(t * LANES, (t + 1) * LANES)
    records = struct_of.shape[0]
    f32, bf16 = jnp.float32, jnp.bfloat16
    me = lax.axis_index("blocks")
    my = lax.axis_index("span")
    zero = lax.div(me, groups)
    near = (me > 0, me < groups - 1, my > 0, my < slabs - 1)
    has = near + tuple(near[a] & near[2 + b] for a in (0, 1) for b in (0, 1))
    step_of = ((-1, 0), (1, 0), (0, -1), (0, 1), (-1, -1), (-1, 1), (1, -1), (1, 1))
    where_to = tuple((me + a, my + b) for a, b in step_of)
    back = (1, 0, 3, 2, 7, 6, 5, 4)

    def at(r, count=SUB):
        if not isinstance(r, int):
            return pl.ds(r, count)
        if r % SUB == 0:
            return slice(r, r + count)
        return pl.ds(zero + r, count)

    def arrived(copies):
        for copy in copies:
            copy.wait()

    barrier = pltpu.get_barrier_semaphore()
    greeted = groups - 1
    for d in range(2, 8):
        greeted = greeted + has[d].astype(jnp.int32)

        @pl.when(has[d])
        def _(d=d):
            pl.semaphore_signal(barrier, inc=1, device_id=where_to[d], device_id_type=MESH)

    for step in range(1, groups):
        pl.semaphore_signal(
            barrier, inc=1, device_id=(lax.rem(me + step, groups), my), device_id_type=MESH
        )

    def load(number, src, dst):
        copies = []
        for t in range(tiles):
            copies.append(
                pltpu.make_async_copy(src(lanes_of(t)), dst(t), sem_in.at[number, t])
            )
            copies[-1].start()
        return copies

    small = [
        pltpu.make_async_copy(src, dst, sem_small.at[n])
        for n, (src, dst) in enumerate(
            (
                (struct_h, struct_of),
                (disp_h, disp),
                (weight_h, weight_of),
                (block_h, block_of),
                (node_h, node_of),
            )
        )
    ]
    for copy in small:
        copy.start()
    load_prior = load(0, lambda x: prior_h.at[:, :, :, x], lambda t: v0.at[:, :, t, own, :])
    load_inv = load(1, lambda x: inv_h.at[:, :, x], lambda t: inv.at[:, t, own, :])
    load_offset = load(2, lambda x: offset_h.at[:, :, :, x], lambda t: sb.at[0:3, :, t, own, :])
    load_vol = load(3, lambda x: vol_h.at[:, :, x], lambda t: sb.at[3, :, t, own, :])
    load_cot = load(4, lambda x: cot_h.at[:, :, :, x], lambda t: adj.at[:, :, t, own, :])

    def flat(ref):
        return ref[...].reshape(1, records)

    arrived(small)
    weights = flat(weight_of)
    onehot_s = (iota((disp.shape[1], records), 0) == flat(struct_of)).astype(bf16)
    parts = jnp.concatenate(split3(disp[...]), axis=0)
    gathered = jnp.dot(parts, onehot_s, preferred_element_type=f32)
    rec_send[0:3, :] = (gathered[0:3] + gathered[3:6] + gathered[6:9]) * weights
    rec_send[3:4, :] = (flat(block_of) * (nj * nk) + flat(node_of)).astype(f32)

    lane = iota((SUB, LANES), 1)
    first_lane, last_lane, left_half = lane == 0, lane == LANES - 1, lane < LANES // 2
    tile_rows = [SUB + r * SUB for r in range(nj // SUB)]

    def pack_lanes(sources, send, column, width):
        per = LANES // width
        chunk = lane // width
        chunk_last = lax.rem(lane + width, LANES) // width
        for g in range(columns(len(sources), width)):
            first = [jnp.zeros((SUB, LANES), f32) for _ in tile_rows]
            last = list(first)
            for p, source in enumerate(sources[g * per : (g + 1) * per]):
                for n, r in enumerate(tile_rows):
                    both = jnp.where(left_half, source(0, r), source(tiles - 1, r))
                    if p:
                        both = pltpu.roll(both, p * width, 1)
                    first[n] = jnp.where(chunk == p, both, first[n])
                    last[n] = jnp.where(chunk_last == p, both, last[n])
            for n in range(len(tile_rows)):
                rows = slice(n * SUB, (n + 1) * SUB)
                send[0, column + g, rows, :] = first[n]
                send[1, column + g, rows, :] = last[n]

    def unpack_lanes(targets, got, column, width, rows):
        per = LANES // width
        chunk = lane // width
        for g in range(columns(len(targets), width)):
            after = [got[0, column + g, at(r), :] for r in rows]
            before = [got[1, column + g, at(r), :] for r in rows]
            for p, target in enumerate(targets[g * per : (g + 1) * per]):
                for n, r in enumerate(rows):
                    both = jnp.where(chunk == p, after[n], before[n])
                    if p:
                        both = pltpu.roll(both, LANES - p * width, 1)
                    target(r, both)

    def edge(ref, *index):
        return lambda t, r: ref[(*index, t, slice(r, r + SUB), slice(None))]

    def halo(ref, *index):
        def put(r, value):
            ref[(*index, tiles, at(r), slice(None))] = value

        return put

    inv_at, second, total_rows = rows_plan(ni)
    field_layers = [(c, i) for c in range(3) for i in range(1, ni)]
    inner = range(1, ni - 1)
    shape_layers = [(c, i) for c in range(4) for i in range(ni)]
    near_columns = columns(len(field_layers) + len(inner), WIDE)

    def take_from(s, count):
        return SUB + s * (nj - count)

    def put_to(s, count):
        return SUB + nj - s * (nj + count)

    def pack_rows(ref, send, start, count, first, stop, unroll, sides=(0, 1)):
        @pl.loop(first, stop, unroll=unroll)
        def _(i):
            for c, source in enumerate(ref):
                for s in sides:
                    for t in range(tiles):
                        spot = pl.ds(start + (c * (stop - first) + i - first) * count, count)
                        send[s, t, spot, :] = source[i, t, at(take_from(s, count), count)]

    def unpack_rows(ref, got, start, count, first, stop, unroll, sides=(0, 1)):
        @pl.loop(first, stop, unroll=unroll)
        def _(i):
            for c, target in enumerate(ref):
                for s in sides:
                    for t in range(tiles):
                        spot = pl.ds(start + (c * (stop - first) + i - first) * count, count)
                        target[i, t, at(put_to(s, count), count)] = got[s, t, spot, :]

    level = [v0, v1, v2, v3, warp]
    field = [level[0].at[c] for c in range(3)]
    shape = [sb.at[c] for c in range(4)]

    def move(d, src, dst, number):
        return pltpu.make_async_remote_copy(
            src_ref=src,
            dst_ref=dst,
            send_sem=sem_halo.at[0, number, d],
            recv_sem=sem_halo.at[1, number, d],
            device_id=where_to[d],
            device_id_type=MESH,
        )

    def start(d, *message):
        @pl.when(has[d])
        def _():
            move(d, *message).start()

    def received(d, *message):
        @pl.when(has[back[d]])
        def _():
            move(d, *message).wait_recv()

    def sent(d, *message):
        @pl.when(has[d])
        def _():
            move(d, *message).wait_send()

    def clear_missing(d, ref):
        @pl.when(jnp.logical_not(has[back[d]]))
        def _():
            ref[...] = jnp.zeros(ref.shape, f32)

    def lane_messages(send, got, number):
        out = []
        for s in (0, 1):
            out.append((2 + s, send.at[s], got.at[s, :, own, :], number))
        for a, rows, to in ((0, slice(0, SUB), end), (1, slice(nj - SUB, nj), top)):
            for s in (0, 1):
                out.append(
                    (4 + 2 * a + s, send.at[s, :, rows, :], got.at[s, :, to, :], number)
                )
        return out

    rows_a = [(d, ja_send.at[d], ja_got.at[d], 0) for d in (0, 1)]
    lanes_a = lane_messages(ka_send, ka_got, 0)
    surf = [(2 + s, v0.at[:, 0, s * (tiles - 1)], surf_got.at[s], 2) for s in (0, 1)]
    rows_c = [(d, jc_send.at[d], jc_got.at[d], 3) for d in (0, 1)]
    lanes_c = lane_messages(kc_send, kc_got, 3)
    def rec_copy(step):
        return pltpu.make_async_remote_copy(
            src_ref=rec_send,
            dst_ref=rec_got.at[me],
            send_sem=sem_rec.at[0, step],
            recv_sem=sem_rec.at[1, step],
            device_id=(lax.rem(me + step, groups), my),
            device_id_type=MESH,
        )

    arrived(load_prior)
    pack_rows(field, ja_send, 0, WIDE, 1, ni, 3)
    arrived(load_inv)
    pack_rows([inv], ja_send, inv_at, SWEEPS, 1, ni - 1, 2)
    arrived(load_offset)
    arrived(load_vol)
    pack_rows(shape, ja_send, second, 1, 0, ni, 2)
    pl.semaphore_wait(barrier, greeted)
    for step in range(1, groups):
        rec_copy(step).start()
    for message in rows_a:
        start(*message)
    pack_lanes(
        [edge(v0, c, i) for c, i in field_layers] + [edge(inv, i) for i in inner],
        ka_send,
        0,
        WIDE,
    )
    pack_lanes([edge(sb, c, i) for c, i in shape_layers], ka_send, near_columns, 1)
    for message in lanes_a:
        start(*message)
    rec_got[me] = rec_send[...]
    for d, _, dst, _ in rows_a + lanes_a + surf + rows_c + lanes_c:
        clear_missing(d, dst)

    def in_pairs(first, stop):
        def run(step):
            unroll = (stop - first) // 2
            even = first + 2 * unroll
            if unroll:
                pl.loop(first, even, unroll=unroll)(step)
            if even < stop:
                step(even)

        return run

    def changes(src, c, i, r, count):
        x = [src[c, i, t, at(r), :] for t in range(every)]
        if count == tiles:
            nexts = [(x[t - 1], x[t], x[(t + 1) % every]) for t in range(tiles)]
            before = [pltpu.roll(jnp.where(last_lane, a, b), 1, 1) for a, b, _ in nexts]
            after = [
                pltpu.roll(jnp.where(first_lane, d, b), LANES - 1, 1) for _, b, d in nexts
            ]
        else:
            right = [pltpu.roll(a, 1, 1) for a in x]
            left = [pltpu.roll(a, LANES - 1, 1) for a in x]
            before = [jnp.where(first_lane, right[t - 1], right[t]) for t in range(every)]
            after = [
                jnp.where(last_lane, left[(t + 1) % every], left[t]) for t in range(every)
            ]
        out = []
        for t in range(count):
            total = before[t] + after[t]
            total = total + (src[c, i, t, at(r - 1), :] + src[c, i, t, at(r + 1), :])
            total = total + (src[c, i - 1, t, at(r), :] + src[c, i + 1, t, at(r), :])
            out.append(total - 6.0 * x[t])
        return x, out

    def sweep_a(s, first, stop, rows):
        src, dst = level[s], level[s + 1]

        @in_pairs(first, stop)
        def _(i):
            for c in range(3):
                for r in rows:
                    x, change = changes(src, c, i, r, every)
                    for t in range(every):
                        dst[c, i, t, at(r), :] = x[t] + inv[i, t, at(r), :] * change[t]

    def keep_layer(i, rows):
        for c in range(3):
            value = level[0][c, i, :, rows, :]
            for s in range(1, SWEEPS + 1):
                level[s][c, i, :, rows, :] = value

    low_row, high_row = SUB - SWEEPS, SUB + nj - SWEEPS
    outer_rows = (low_row, high_row)
    shifted_rows = list(range(low_row, high_row + 1, SUB))
    field_halos = [halo(v0, c, i) for c, i in field_layers] + [halo(inv, i) for i in inner]
    shape_halos = [halo(sb, c, i) for c, i in shape_layers]

    def target_of(code):
        row = jnp.floor((code + 0.5) * (1.0 / nk))
        return row, code - row * nk

    together = 2 if groups % 2 == 0 and records <= 4 * LANES else 1

    def side_by_side(parts):
        return parts[0] if len(parts) == 1 else jnp.concatenate(parts, axis=1)

    row_of = (me * nj + iota((all_rows, together * records), 0) - SUB).astype(f32)
    col_of = iota((nk, together * records), 0).astype(f32)

    def scatter(members, total):
        got = side_by_side([rec_got[g] for g in members])
        row, col = target_of(got[3:4, :])
        here = row_of == row
        cols = (col_of == col).astype(bf16)
        pieces = split3(got[0:3, :])
        left = jnp.concatenate(
            [
                jnp.where(here, pieces[n][c : c + 1, :].astype(f32), 0.0)
                for n in range(3)
                for c in range(3)
            ],
            axis=0,
        ).astype(bf16)
        out = lax.dot_general(
            left, cols, (((1,), (1,)), ((), ())), preferred_element_type=f32
        )
        rows = 3 * all_rows
        return total + (out[0:rows] + out[rows : 2 * rows] + out[2 * rows :])

    def scatter_next(n, total):
        steps = [n * together + k for k in range(together)]
        for step in steps:
            rec_copy(step).wait_recv()
        return scatter([lax.rem(me - step + groups, groups) for step in steps], total)

    for step in range(1, together):
        rec_copy(step).wait_recv()
    surface = scatter(
        [lax.rem(me - step + groups, groups) for step in range(together)],
        jnp.zeros((3 * all_rows, nk), f32),
    )
    surface = lax.fori_loop(1, groups // together, scatter_next, surface)
    for c in range(3):
        for t in range(tiles):
            v0[c, 0, t] = surface[c * all_rows : (c + 1) * all_rows, lanes_of(t)]
    for message in surf:
        start(*message)

    for message in lanes_a[:2]:
        received(*message)
    unpack_lanes(field_halos, ka_got, 0, WIDE, tile_rows)
    keep_layer(ni - 1, own)
    for s in range(SWEEPS):
        sweep_a(s, s + 2, ni - 1, tile_rows)

    def either(s, values):
        return ((s == 0) & values[0]) | ((s == 1) & values[1])

    def side_copy(s, send, got, number):
        return pltpu.make_async_remote_copy(
            src_ref=send.at[s],
            dst_ref=got.at[s],
            send_sem=sem_halo.at[0, number, s],
            recv_sem=sem_halo.at[1, number, s],
            device_id=(me - 1 + 2 * s, my),
            device_id_type=MESH,
        )

    def corner_copy(s, b):
        d = 4 + 2 * s + b
        return pltpu.make_async_remote_copy(
            src_ref=ka_send.at[b, :, pl.ds(pl.multiple_of(s * (nj - SUB), SUB), SUB), :],
            dst_ref=ka_got.at[b, :, pl.ds(corner_row(s), SUB), :],
            send_sem=sem_halo.at[0, 0, d],
            recv_sem=sem_halo.at[1, 0, d],
            device_id=(me - 1 + 2 * s, my - 1 + 2 * b),
            device_id_type=MESH,
        )

    def corner_row(s):
        return pl.multiple_of((1 - s) * (SUB + nj), SUB)

    def outer_row(s):
        return low_row + (1 - s) * (high_row - low_row)

    def outer(s):
        comes = either(s, (near[1], near[0]))

        @pl.when(comes)
        def _():
            side_copy(s, ja_send, ja_got, 0).wait_recv()

        for b in (0, 1):

            @pl.when(comes & near[3 - b])
            def _(b=b):
                corner_copy(s, b).wait_recv()

        unpack_rows(field, ja_got, 0, WIDE, 1, ni, 3, (s,))
        unpack_rows([inv], ja_got, inv_at, SWEEPS, 1, ni - 1, 2, (s,))
        unpack_lanes(field_halos, ka_got, 0, WIDE, (corner_row(s),))
        unpack_rows(shape, ja_got, second, 1, 0, ni, 2, (s,))
        unpack_lanes(shape_halos, ka_got, near_columns, 1, (corner_row(s),))
        keep_layer(ni - 1, pl.ds(corner_row(s), SUB))

    def shape_rows(rows):
        for r in rows:
            row_at = me * nj + iota((SUB, LANES), 0) + (r - SUB)
            row_in = (row_at >= 0) & (row_at < groups * nj - 1)
            for t in range(every):
                col_at = my * nk + lane + (t * LANES if t < tiles else -LANES)
                cell = row_in & (col_at >= 0) & (col_at < slabs * nk - 1)

                @pl.loop(0, ni, unroll=4)
                def _(i, r=r, t=t, cell=cell):
                    for c in range(3):
                        sb[c, i, t, at(r), :] = sb[c, i, t, at(r), :] + warp[c, i, t, at(r), :]
                    keep = cell & (i < ni - 1)
                    sb[3, i, t, at(r), :] = jnp.where(keep, sb[3, i, t, at(r), :], 0.0)

    later = lax.rem(me, 2)
    sooner = 1 - later
    outer(sooner)
    for s in range(SWEEPS):
        sweep_a(s, s + 2, ni - 1, (outer_row(sooner),))

    unpack_lanes(shape_halos, ka_got, near_columns, 1, tile_rows)
    for message in surf:
        received(*message)
    for c in range(3):
        for r in range(0, all_rows, SUB):
            rows = slice(r, r + SUB)
            v0[c, 0, tiles, rows, :] = jnp.where(
                left_half, surf_got[0, c, rows, :], surf_got[1, c, rows, :]
            )
    keep_layer(0, slice(0, all_rows))
    for s in range(SWEEPS):
        sweep_a(s, 1, s + 2, tile_rows + [outer_row(sooner)])

    def cross(a, b):
        return (
            a[1] * b[2] - a[2] * b[1],
            a[2] * b[0] - a[0] * b[2],
            a[0] * b[1] - a[1] * b[0],
        )

    low_i[...] = jnp.zeros(low_i.shape, f32)
    arrived(load_cot)

    def gradients(parts):
        @pl.loop(0, ni, unroll=2)
        def _(i):
            above = jnp.minimum(i + 1, ni - 1)
            for r, full in parts:
                order = (tiles, *range(tiles)) if full else range(tiles)
                base = [[sb[c, i, t, at(r), :] for c in range(3)] for t in range(every)]
                held = None
                for t in order:
                    edge_i = [sb[c, above, t, at(r), :] - base[t][c] for c in range(3)]
                    edge_i[0] = edge_i[0] + 1.0
                    weight = sb[3, i, t, at(r), :]
                    weighted_i = [weight * e for e in edge_i]
                    if full:
                        edge_j = [sb[c, i, t, at(r + 1), :] - base[t][c] for c in range(3)]
                        edge_j[1] = edge_j[1] + 1.0
                        grad_k = cross(weighted_i, edge_j)
                    if t < tiles:
                        follow = base[(t + 1) % every]
                        edge_k = [
                            pltpu.roll(
                                jnp.where(first_lane, follow[c], base[t][c]), LANES - 1, 1
                            )
                            - base[t][c]
                            for c in range(3)
                        ]
                        edge_k[2] = edge_k[2] + 1.0
                        grad_j = cross(edge_k, weighted_i)
                        for c in range(3):
                            low_j[c, t, at(r), :] = grad_j[c]
                    if full and t < tiles:
                        grad_i = cross([weight * e for e in edge_j], edge_k)
                        rate = jnp.where((i > 0) & (i < ni - 1), inv[i, t, at(r), :], 0.0)
                        for c in range(3):
                            lower_k = pltpu.roll(
                                jnp.where(last_lane, held[c], grad_k[c]), 1, 1
                            )
                            out = adj[c, i, t, at(r), :] - grad_i[c] + low_i[c, t, at(r), :]
                            out = out + (low_j[c, t, at(r - 1), :] - grad_j[c])
                            out = out + (lower_k - grad_k[c])
                            low_i[c, t, at(r), :] = grad_i[c]
                            adj[c, i, t, at(r), :] = out
                            v0[c, i, t, at(r), :] = rate * out
                    if full:
                        held = grad_k

    flux_layers = [(c, i) for c in range(3) for i in inner]

    def send_flux(s):
        pack_rows(field, jc_send, 0, SWEEPS, 1, ni - 1, 2, (s,))

        @pl.when(either(s, near[:2]))
        def _():
            side_copy(s, jc_send, jc_got, 3).start()

    for message in surf:
        sent(*message)
    count = len(tile_rows)
    shape_rows([low_row + (1 - sooner) * SUB + n * SUB for n in range(count)])
    gradients([((1 - sooner) * SUB + n * SUB, n > 0) for n in range(count)])
    send_flux(later)

    outer(later)
    for s in range(SWEEPS):
        sweep_a(s, 1, ni - 1, (outer_row(later),))
    shape_rows([outer_row(later)])
    gradients([((1 - later) * (nj - SUB) + n * SUB, n > 0) for n in range(2)])
    send_flux(sooner)
    pack_lanes([edge(v0, c, i) for c, i in flux_layers], kc_send, 0, SWEEPS)
    for message in lanes_c:
        start(*message)
    for s in range(SWEEPS):
        for c in range(3):
            for i in (0, ni - 1):
                level[s][c, i] = jnp.zeros(v0.shape[2:], f32)

    def sweep_c(s, first, stop, rows, adds):
        src = level[s]
        last = s == SWEEPS - 1

        @in_pairs(first, stop)
        def _(i):
            for c in range(3):
                for r, (low, high) in zip(rows, adds):
                    x, change = changes(src, c, i, r, tiles if last else every)
                    for t, delta in enumerate(change):
                        if t < tiles:
                            to = at(r + low, high - low)
                            adj[c, i, t, to, :] = adj[c, i, t, to, :] + delta[low:high]
                        if not last:
                            level[s + 1][c, i, t, at(r), :] = (
                                x[t] + inv[i, t, at(r), :] * delta
                            )

    whole = (0, SUB)
    flux_halos = [halo(v0, c, i) for c, i in flux_layers]
    for message in lanes_c[:2]:
        received(*message)
    unpack_lanes(flux_halos, kc_got, 0, SWEEPS, tile_rows)
    inner_adds = [whole] * len(tile_rows)
    inner_adds[0] = (SWEEPS, SUB)
    inner_adds[-1] = (0, SUB - SWEEPS)
    for s in range(SWEEPS - 1):
        sweep_c(s, 1, ni - 1, tile_rows, inner_adds)
    mid_rows = shifted_rows[1:-1]
    sweep_c(SWEEPS - 1, 1, ni - 1, mid_rows, [whole] * len(mid_rows))

    for message in rows_c + lanes_c[2:]:
        received(*message)
    unpack_rows(field, jc_got, 0, SWEEPS, 1, ni - 1, 2)
    unpack_lanes(flux_halos, kc_got, 0, SWEEPS, (0, SUB + nj))
    for s in range(SWEEPS - 1):
        sweep_c(s, 1, SWEEPS - s, outer_rows, [whole] * 2)

    def add_wall(wall, layer):
        for c in range(3):
            for t in range(tiles):
                for r in tile_rows:
                    value = adj[c, wall, t, at(r), :]
                    for s in range(SWEEPS):
                        value = value + level[s][c, layer, t, at(r), :]
                    adj[c, wall, t, at(r), :] = value

    add_wall(0, 1)

    def wall_of(c):
        return jnp.concatenate([adj[c, 0, t, own, :] for t in range(tiles)], axis=1)

    wall = jnp.concatenate(
        [jnp.concatenate(split3(wall_of(c)), axis=0) for c in range(3)], axis=0
    )
    row_w = (me * nj + iota((nj, together * records), 0)).astype(f32)

    def reply_copy(step):
        to = lax.rem(me + step, groups)
        return pltpu.make_async_remote_copy(
            src_ref=reply_send.at[to],
            dst_ref=reply_got.at[me],
            send_sem=sem_reply.at[0, step],
            recv_sem=sem_reply.at[1, step],
            device_id=(to, my),
            device_id_type=MESH,
        )

    def answer(members):
        row, col = target_of(side_by_side([rec_got[g, 3:4, :] for g in members]))
        cols = (col_of == col).astype(bf16)
        here = row_w == row
        out = jnp.dot(wall, cols, preferred_element_type=f32)
        for c in range(3):
            first = 3 * c * nj
            value = (
                out[first : first + nj]
                + out[first + nj : first + 2 * nj]
                + out[first + 2 * nj : first + 3 * nj]
            )
            found = jnp.sum(jnp.where(here, value, 0.0), axis=0, keepdims=True)
            for n, g in enumerate(members):
                reply_send[g, c : c + 1, :] = found[:, n * records : (n + 1) * records]
        for g in members:
            reply_send[g, 3:4, :] = jnp.zeros((1, records), f32)

    def answer_next(n, last):
        steps = [n * together + k + 1 for k in range(together)]
        answer([lax.rem(me + step, groups) for step in steps])
        for step in steps[: together - 1] if last else steps:
            reply_copy(step).start()

    @pl.loop(0, groups // together - 1)
    def _(n):
        answer_next(n, False)

    answer_next(groups // together - 1, True)
    reply_got[me] = reply_send[me]

    for s in range(SWEEPS - 1):
        sweep_c(s, SWEEPS - s, ni - 1, outer_rows, [whole] * 2)
    sweep_c(SWEEPS - 1, 1, ni - 1, outer_rows, [whole] * 2)
    add_wall(ni - 1, ni - 2)

    for step in range(1, groups):
        reply_copy(step).wait_recv()
    total = lax.fori_loop(
        0, groups, lambda g, kept: kept + reply_got[g], jnp.zeros((4, records), f32)
    )
    weighted = jnp.concatenate(split3(total[0:3] * weights), axis=0)
    out = lax.dot_general(
        weighted, onehot_s, (((1,), (1,)), ((), ())), preferred_element_type=f32
    )
    sens_o[...] = out[0:3] + out[3:6] + out[6:9]
    for message in rows_a + lanes_a + rows_c + lanes_c:
        sent(*message)
    for step in range(1, groups):
        reply_copy(step).wait_send()
        rec_copy(step).wait_send()


def deliver(warp, adj, sens, warp_h, adj_h, sens_h, sem):
    nj, nk = warp_h.shape[2:]
    own = slice(SUB, SUB + nj)
    copies = []
    for n, (src, dst) in enumerate(((warp, warp_h), (adj, adj_h))):
        for c in range(3):
            for t in range(nk // LANES):
                lanes = slice(t * LANES, (t + 1) * LANES)
                copies.append(
                    pltpu.make_async_copy(
                        src.at[c, :, t, own, :], dst.at[c, :, :, lanes], sem.at[n, c, t]
                    )
                )
                copies[-1].start()
    sens_h[...] = sens[...]
    for copy in copies:
        copy.wait()


def body(
    struct_disp,
    rec_struct,
    rec_block,
    rec_node,
    rec_weight,
    offset,
    prior_warp,
    inv_volume,
    coord_cot,
    vol_cot,
):
    groups = lax.axis_size("blocks")
    slabs = lax.axis_size("span")
    _, ni, nj, nk = offset.shape
    records = rec_struct.shape[0]
    f32 = jnp.float32
    all_rows = nj + 2 * SUB
    tiles = nk // LANES
    _, _, total_rows = rows_plan(ni)
    cols_a = columns(3 * (ni - 1) + ni - 2, WIDE) + columns(4 * ni, 1)
    cols_c = columns(3 * (ni - 2), SWEEPS)
    rows_c = -(-3 * (ni - 2) * SWEEPS // SUB) * SUB

    def lane_buffers(count):
        return [
            pltpu.VMEM((2, count, nj, LANES), f32),
            pltpu.VMEM((2, count, all_rows, LANES), f32),
        ]

    vmem = pl.BlockSpec(memory_space=pltpu.VMEM)
    hbm = pl.BlockSpec(memory_space=pltpu.HBM)
    in_place = lambda x: pltpu.with_memory_space_constraint(x, pltpu.HBM)
    warp, adj, sens = pl.pallas_call(
        functools.partial(kernel, groups, slabs),
        out_shape=(
            pltpu.VMEM((3, ni, tiles + 1, all_rows, LANES), f32),
            pltpu.VMEM((3, ni, tiles, all_rows, LANES), f32),
            pltpu.VMEM(struct_disp.shape, f32),
        ),
        in_specs=[hbm] * 10,
        out_specs=[vmem] * 3,
        scratch_shapes=[
            *([pltpu.VMEM((3, ni, tiles + 1, all_rows, LANES), f32)] * SWEEPS),
            pltpu.VMEM((ni, tiles + 1, all_rows, LANES), f32),
            pltpu.VMEM((4, ni, tiles + 1, all_rows, LANES), f32),
            pltpu.VMEM((3, tiles, nj + SUB, LANES), f32),
            pltpu.VMEM((3, tiles, nj + SUB, LANES), f32),
            pltpu.VMEM((4, records), f32),
            pltpu.VMEM((groups, 4, records), f32),
            pltpu.VMEM((groups, 4, records), f32),
            pltpu.VMEM((groups, 4, records), f32),
            *([pltpu.VMEM((2, tiles, total_rows, LANES), f32)] * 2),
            *lane_buffers(cols_a),
            pltpu.VMEM((2, 3, all_rows, LANES), f32),
            *([pltpu.VMEM((2, tiles, rows_c, LANES), f32)] * 2),
            *lane_buffers(cols_c),
            *([pltpu.VMEM((records,), jnp.int32)] * 3),
            pltpu.VMEM((records,), f32),
            pltpu.VMEM(struct_disp.shape, f32),
            pltpu.SemaphoreType.DMA((5,)),
            pltpu.SemaphoreType.DMA((2, groups)),
            pltpu.SemaphoreType.DMA((2, groups)),
            pltpu.SemaphoreType.DMA((2, 4, 8)),
            pltpu.SemaphoreType.DMA((5, tiles)),
        ],
        compiler_params=pltpu.CompilerParams(
            collective_id=0, has_side_effects=True, vmem_limit_bytes=VMEM_LIMIT
        ),
        name="warp_adjoint",
    )(
        *map(
            in_place,
            (
                rec_struct,
                rec_block.reshape(records),
                rec_node,
                rec_weight,
                struct_disp,
                offset,
                prior_warp,
                inv_volume,
                coord_cot,
                vol_cot,
            ),
        )
    )
    return pl.pallas_call(
        deliver,
        out_shape=(
            jax.ShapeDtypeStruct(offset.shape, f32),
            jax.ShapeDtypeStruct(offset.shape, f32),
            jax.ShapeDtypeStruct(struct_disp.shape, f32),
        ),
        in_specs=[vmem] * 3,
        out_specs=[hbm, hbm, vmem],
        scratch_shapes=[pltpu.SemaphoreType.DMA((2, 3, tiles))],
        compiler_params=pltpu.CompilerParams(vmem_limit_bytes=4 * 1024 * 1024),
        name="deliver",
    )(warp, adj, sens)


def solution(mesh):
    placed = (
        P(None, ("blocks", "span")),
        P(("blocks", "span")),
        P(("blocks", "span"), None),
        P(("blocks", "span")),
        P(("blocks", "span")),
        P(None, None, "blocks", "span"),
        P(None, None, "blocks", "span"),
        P(None, "blocks", "span"),
        P(None, None, "blocks", "span"),
        P(None, "blocks", "span"),
    )
    return jax.shard_map(
        body,
        mesh=mesh,
        in_specs=placed,
        out_specs=(
            P(None, None, "blocks", "span"),
            P(None, None, "blocks", "span"),
            P(None, ("blocks", "span")),
        ),
        check_vma=False,
    )
```

```python
import functools

import jax
import jax.numpy as jnp
from jax import lax
from jax.experimental import pallas as pl
from jax.experimental.pallas import tpu as pltpu
from jax.sharding import PartitionSpec as P

SWEEPS = 4
WIDE = SWEEPS + 1
LANES = 128
SUB = 8
VMEM_LIMIT = 40 * 1024 * 1024
MESH = pl.DeviceIdType.MESH


def split3(x):
    hi = x.astype(jnp.bfloat16)
    rest = x - hi.astype(jnp.float32)
    mid = rest.astype(jnp.bfloat16)
    low = (rest - mid.astype(jnp.float32)).astype(jnp.bfloat16)
    return hi, mid, low


def iota(shape, dim):
    return lax.broadcasted_iota(jnp.int32, shape, dim)


def rows_plan(ni):
    inv = 3 * (ni - 1) * WIDE
    second = -(-(inv + (ni - 2) * SWEEPS) // SUB) * SUB
    total = second + -(-4 * ni // SUB) * SUB
    return inv, second, total


def columns(chunks, width):
    return -(-chunks // (LANES // width))


def kernel(
    groups,
    slabs,
    struct_h,
    block_h,
    node_h,
    weight_h,
    disp_h,
    offset_h,
    prior_h,
    inv_h,
    cot_h,
    vol_h,
    warp,
    adj,
    sens_o,
    v0,
    v1,
    v2,
    v3,
    inv,
    sb,
    low_i,
    low_j,
    rec_send,
    rec_got,
    reply_send,
    reply_got,
    ja_send,
    ja_got,
    ka_send,
    ka_got,
    surf_got,
    jc_send,
    jc_got,
    kc_send,
    kc_got,
    struct_of,
    block_of,
    node_of,
    weight_of,
    disp,
    sem_small,
    sem_rec,
    sem_reply,
    sem_halo,
    sem_in,
):
    ni, nj, nk = offset_h.shape[1:]
    tiles = nk // LANES
    every = tiles + 1
    own = slice(SUB, SUB + nj)
    top, end = slice(0, SUB), slice(SUB + nj, SUB + nj + SUB)
    all_rows = nj + 2 * SUB
    lanes_of = lambda t: slice(t * LANES, (t + 1) * LANES)
    records = struct_of.shape[0]
    f32, bf16 = jnp.float32, jnp.bfloat16
    me = lax.axis_index("blocks")
    my = lax.axis_index("span")
    zero = lax.div(me, groups)
    near = (me > 0, me < groups - 1, my > 0, my < slabs - 1)
    has = near + tuple(near[a] & near[2 + b] for a in (0, 1) for b in (0, 1))
    step_of = ((-1, 0), (1, 0), (0, -1), (0, 1), (-1, -1), (-1, 1), (1, -1), (1, 1))
    where_to = tuple((me + a, my + b) for a, b in step_of)
    back = (1, 0, 3, 2, 7, 6, 5, 4)

    def at(r, count=SUB):
        if not isinstance(r, int):
            return pl.ds(r, count)
        if r % SUB == 0:
            return slice(r, r + count)
        return pl.ds(zero + r, count)

    def arrived(copies):
        for copy in copies:
            copy.wait()

    barrier = pltpu.get_barrier_semaphore()
    greeted = groups - 1
    for d in range(2, 8):
        greeted = greeted + has[d].astype(jnp.int32)

        @pl.when(has[d])
        def _(d=d):
            pl.semaphore_signal(barrier, inc=1, device_id=where_to[d], device_id_type=MESH)

    for step in range(1, groups):
        pl.semaphore_signal(
            barrier, inc=1, device_id=(lax.rem(me + step, groups), my), device_id_type=MESH
        )

    def load(number, src, dst):
        copies = []
        for t in range(tiles):
            copies.append(
                pltpu.make_async_copy(src(lanes_of(t)), dst(t), sem_in.at[number, t])
            )
            copies[-1].start()
        return copies

    small = [
        pltpu.make_async_copy(src, dst, sem_small.at[n])
        for n, (src, dst) in enumerate(
            (
                (struct_h, struct_of),
                (disp_h, disp),
                (weight_h, weight_of),
                (block_h, block_of),
                (node_h, node_of),
            )
        )
    ]
    for copy in small:
        copy.start()
    load_prior = load(0, lambda x: prior_h.at[:, :, :, x], lambda t: v0.at[:, :, t, own, :])
    load_inv = load(1, lambda x: inv_h.at[:, :, x], lambda t: inv.at[:, t, own, :])
    load_offset = load(2, lambda x: offset_h.at[:, :, :, x], lambda t: sb.at[0:3, :, t, own, :])
    load_vol = load(3, lambda x: vol_h.at[:, :, x], lambda t: sb.at[3, :, t, own, :])
    load_cot = load(4, lambda x: cot_h.at[:, :, :, x], lambda t: adj.at[:, :, t, own, :])

    def flat(ref):
        return ref[...].reshape(1, records)

    arrived(small)
    weights = flat(weight_of)
    onehot_s = (iota((disp.shape[1], records), 0) == flat(struct_of)).astype(bf16)
    parts = jnp.concatenate(split3(disp[...]), axis=0)
    gathered = jnp.dot(parts, onehot_s, preferred_element_type=f32)
    rec_send[0:3, :] = (gathered[0:3] + gathered[3:6] + gathered[6:9]) * weights
    rec_send[3:4, :] = (flat(block_of) * (nj * nk) + flat(node_of)).astype(f32)

    lane = iota((SUB, LANES), 1)
    first_lane, last_lane, left_half = lane == 0, lane == LANES - 1, lane < LANES // 2
    tile_rows = [SUB + r * SUB for r in range(nj // SUB)]

    def pack_lanes(sources, send, column, width, tiles_at):
        per = LANES // width
        chunk = lane // width
        chunk_last = lax.rem(lane + width, LANES) // width
        for g in range(columns(len(sources), width)):
            first = [jnp.zeros((SUB, LANES), f32) for _ in tiles_at]
            last = list(first)
            for p, source in enumerate(sources[g * per : (g + 1) * per]):
                for n, r in enumerate(tiles_at):
                    both = jnp.where(left_half, source(0, r), source(tiles - 1, r))
                    if p:
                        both = pltpu.roll(both, p * width, 1)
                    first[n] = jnp.where(chunk == p, both, first[n])
                    last[n] = jnp.where(chunk_last == p, both, last[n])
            for n, r in enumerate(tiles_at):
                send[0, column + g, at(r - SUB), :] = first[n]
                send[1, column + g, at(r - SUB), :] = last[n]

    def unpack_lanes(targets, got, column, width, rows):
        per = LANES // width
        chunk = lane // width
        for g in range(columns(len(targets), width)):
            after = [got[0, column + g, at(r), :] for r in rows]
            before = [got[1, column + g, at(r), :] for r in rows]
            for p, target in enumerate(targets[g * per : (g + 1) * per]):
                for n, r in enumerate(rows):
                    both = jnp.where(chunk == p, after[n], before[n])
                    if p:
                        both = pltpu.roll(both, LANES - p * width, 1)
                    target(r, both)

    def edge(ref, *index):
        return lambda t, r: ref[(*index, t, at(r), slice(None))]

    def halo(ref, *index):
        def put(r, value):
            ref[(*index, tiles, at(r), slice(None))] = value

        return put

    inv_at, second, total_rows = rows_plan(ni)
    field_layers = [(c, i) for c in range(3) for i in range(1, ni)]
    inner = range(1, ni - 1)
    shape_layers = [(c, i) for c in range(4) for i in range(ni)]
    near_columns = columns(len(field_layers) + len(inner), WIDE)

    def take_from(s, count):
        return SUB + s * (nj - count)

    def put_to(s, count):
        return SUB + nj - s * (nj + count)

    def pack_rows(ref, send, start, count, first, stop, unroll, sides=(0, 1)):
        @pl.loop(first, stop, unroll=unroll)
        def _(i):
            for c, source in enumerate(ref):
                for s in sides:
                    for t in range(tiles):
                        spot = pl.ds(start + (c * (stop - first) + i - first) * count, count)
                        send[s, t, spot, :] = source[i, t, at(take_from(s, count), count)]

    def unpack_rows(ref, got, start, count, first, stop, unroll, sides=(0, 1)):
        @pl.loop(first, stop, unroll=unroll)
        def _(i):
            for c, target in enumerate(ref):
                for s in sides:
                    for t in range(tiles):
                        spot = pl.ds(start + (c * (stop - first) + i - first) * count, count)
                        target[i, t, at(put_to(s, count), count)] = got[s, t, spot, :]

    level = [v0, v1, v2, v3, warp]
    field = [level[0].at[c] for c in range(3)]
    shape = [sb.at[c] for c in range(4)]

    def move(d, src, dst, number):
        return pltpu.make_async_remote_copy(
            src_ref=src,
            dst_ref=dst,
            send_sem=sem_halo.at[0, number, d],
            recv_sem=sem_halo.at[1, number, d],
            device_id=where_to[d],
            device_id_type=MESH,
        )

    def start(d, *message):
        @pl.when(has[d])
        def _():
            move(d, *message).start()

    def received(d, *message):
        @pl.when(has[back[d]])
        def _():
            move(d, *message).wait_recv()

    def sent(d, *message):
        @pl.when(has[d])
        def _():
            move(d, *message).wait_send()

    def clear_missing(d, ref):
        @pl.when(jnp.logical_not(has[back[d]]))
        def _():
            ref[...] = jnp.zeros(ref.shape, f32)

    def lane_messages(send, got, number):
        out = []
        for s in (0, 1):
            out.append((2 + s, send.at[s], got.at[s, :, own, :], number))
        for a, rows, to in ((0, slice(0, SUB), end), (1, slice(nj - SUB, nj), top)):
            for s in (0, 1):
                out.append(
                    (4 + 2 * a + s, send.at[s, :, rows, :], got.at[s, :, to, :], number)
                )
        return out

    rows_a = [(d, ja_send.at[d], ja_got.at[d], 0) for d in (0, 1)]
    lanes_a = lane_messages(ka_send, ka_got, 0)
    surf = [(2 + s, v0.at[:, 0, s * (tiles - 1)], surf_got.at[s], 2) for s in (0, 1)]
    rows_c = [(d, jc_send.at[d], jc_got.at[d], 3) for d in (0, 1)]
    lanes_c = lane_messages(kc_send, kc_got, 3)[2:]
    def rec_copy(step):
        return pltpu.make_async_remote_copy(
            src_ref=rec_send,
            dst_ref=rec_got.at[me],
            send_sem=sem_rec.at[0, step],
            recv_sem=sem_rec.at[1, step],
            device_id=(lax.rem(me + step, groups), my),
            device_id_type=MESH,
        )

    arrived(load_prior)
    pack_rows(field, ja_send, 0, WIDE, 1, ni, 3)
    arrived(load_inv)
    pack_rows([inv], ja_send, inv_at, SWEEPS, 1, ni - 1, 2)
    arrived(load_offset)
    arrived(load_vol)
    pack_rows(shape, ja_send, second, 1, 0, ni, 2)
    pl.semaphore_wait(barrier, greeted)
    for step in range(1, groups):
        rec_copy(step).start()
    for message in rows_a:
        start(*message)
    pack_lanes(
        [edge(v0, c, i) for c, i in field_layers] + [edge(inv, i) for i in inner],
        ka_send,
        0,
        WIDE,
        tile_rows,
    )
    pack_lanes([edge(sb, c, i) for c, i in shape_layers], ka_send, near_columns, 1, tile_rows)
    for message in lanes_a:
        start(*message)
    rec_got[me] = rec_send[...]
    for d, _, dst, _ in rows_a + lanes_a + surf + rows_c + lanes_c:
        clear_missing(d, dst)
    for s in (0, 1):
        clear_missing(2 + s, kc_got.at[s, :, own, :])

    def in_pairs(first, stop):
        def run(step):
            unroll = (stop - first) // 2
            even = first + 2 * unroll
            if unroll:
                pl.loop(first, even, unroll=unroll)(step)
            if even < stop:
                step(even)

        return run

    def changes(src, c, i, r, count):
        x = [src[c, i, t, at(r), :] for t in range(every)]
        if count == tiles:
            nexts = [(x[t - 1], x[t], x[(t + 1) % every]) for t in range(tiles)]
            before = [pltpu.roll(jnp.where(last_lane, a, b), 1, 1) for a, b, _ in nexts]
            after = [
                pltpu.roll(jnp.where(first_lane, d, b), LANES - 1, 1) for _, b, d in nexts
            ]
        else:
            right = [pltpu.roll(a, 1, 1) for a in x]
            left = [pltpu.roll(a, LANES - 1, 1) for a in x]
            before = [jnp.where(first_lane, right[t - 1], right[t]) for t in range(every)]
            after = [
                jnp.where(last_lane, left[(t + 1) % every], left[t]) for t in range(every)
            ]
        out = []
        for t in range(count):
            total = before[t] + after[t]
            total = total + (src[c, i, t, at(r - 1), :] + src[c, i, t, at(r + 1), :])
            total = total + (src[c, i - 1, t, at(r), :] + src[c, i + 1, t, at(r), :])
            out.append(total - 6.0 * x[t])
        return x, out

    def sweep_a(s, first, stop, rows):
        src, dst = level[s], level[s + 1]

        @in_pairs(first, stop)
        def _(i):
            for c in range(3):
                for r in rows:
                    x, change = changes(src, c, i, r, every)
                    for t in range(every):
                        dst[c, i, t, at(r), :] = x[t] + inv[i, t, at(r), :] * change[t]

    def keep_layer(i, rows):
        for c in range(3):
            value = level[0][c, i, :, rows, :]
            for s in range(1, SWEEPS + 1):
                level[s][c, i, :, rows, :] = value

    low_row, high_row = SUB - SWEEPS, SUB + nj - SWEEPS
    outer_rows = (low_row, high_row)
    shifted_rows = list(range(low_row, high_row + 1, SUB))
    field_halos = [halo(v0, c, i) for c, i in field_layers] + [halo(inv, i) for i in inner]
    shape_halos = [halo(sb, c, i) for c, i in shape_layers]

    def target_of(code):
        row = jnp.floor((code + 0.5) * (1.0 / nk))
        return row, code - row * nk

    together = 2 if groups % 2 == 0 and records <= 4 * LANES else 1

    def side_by_side(parts):
        return parts[0] if len(parts) == 1 else jnp.concatenate(parts, axis=1)

    row_of = (me * nj + iota((all_rows, together * records), 0) - SUB).astype(f32)
    col_of = iota((nk, together * records), 0).astype(f32)

    def scatter(members, total):
        got = side_by_side([rec_got[g] for g in members])
        row, col = target_of(got[3:4, :])
        here = row_of == row
        cols = (col_of == col).astype(bf16)
        pieces = split3(got[0:3, :])
        left = jnp.concatenate(
            [
                jnp.where(here, pieces[n][c : c + 1, :].astype(f32), 0.0)
                for n in range(3)
                for c in range(3)
            ],
            axis=0,
        ).astype(bf16)
        out = lax.dot_general(
            left, cols, (((1,), (1,)), ((), ())), preferred_element_type=f32
        )
        rows = 3 * all_rows
        return total + (out[0:rows] + out[rows : 2 * rows] + out[2 * rows :])

    def scatter_next(n, total):
        steps = [n * together + k for k in range(together)]
        for step in steps:
            rec_copy(step).wait_recv()
        return scatter([lax.rem(me - step + groups, groups) for step in steps], total)

    for step in range(1, together):
        rec_copy(step).wait_recv()
    surface = scatter(
        [lax.rem(me - step + groups, groups) for step in range(together)],
        jnp.zeros((3 * all_rows, nk), f32),
    )
    surface = lax.fori_loop(1, groups // together, scatter_next, surface)
    for c in range(3):
        for t in range(tiles):
            v0[c, 0, t] = surface[c * all_rows : (c + 1) * all_rows, lanes_of(t)]
    for message in surf:
        start(*message)

    for message in lanes_a[:2]:
        received(*message)
    unpack_lanes(field_halos, ka_got, 0, WIDE, tile_rows)
    keep_layer(ni - 1, own)
    for s in range(SWEEPS):
        sweep_a(s, s + 2, ni - 1, tile_rows)

    def either(s, values):
        return ((s == 0) & values[0]) | ((s == 1) & values[1])

    def side_copy(s, send, got, number):
        return pltpu.make_async_remote_copy(
            src_ref=send.at[s],
            dst_ref=got.at[s],
            send_sem=sem_halo.at[0, number, s],
            recv_sem=sem_halo.at[1, number, s],
            device_id=(me - 1 + 2 * s, my),
            device_id_type=MESH,
        )

    def corner_copy(s, b):
        d = 4 + 2 * s + b
        return pltpu.make_async_remote_copy(
            src_ref=ka_send.at[b, :, pl.ds(pl.multiple_of(s * (nj - SUB), SUB), SUB), :],
            dst_ref=ka_got.at[b, :, pl.ds(corner_row(s), SUB), :],
            send_sem=sem_halo.at[0, 0, d],
            recv_sem=sem_halo.at[1, 0, d],
            device_id=(me - 1 + 2 * s, my - 1 + 2 * b),
            device_id_type=MESH,
        )

    def corner_row(s):
        return pl.multiple_of((1 - s) * (SUB + nj), SUB)

    def outer_row(s):
        return low_row + (1 - s) * (high_row - low_row)

    def outer(s):
        comes = either(s, (near[1], near[0]))

        @pl.when(comes)
        def _():
            side_copy(s, ja_send, ja_got, 0).wait_recv()

        for b in (0, 1):

            @pl.when(comes & near[3 - b])
            def _(b=b):
                corner_copy(s, b).wait_recv()

        unpack_rows(field, ja_got, 0, WIDE, 1, ni, 3, (s,))
        unpack_rows([inv], ja_got, inv_at, SWEEPS, 1, ni - 1, 2, (s,))
        unpack_lanes(field_halos, ka_got, 0, WIDE, (corner_row(s),))
        unpack_rows(shape, ja_got, second, 1, 0, ni, 2, (s,))
        unpack_lanes(shape_halos, ka_got, near_columns, 1, (corner_row(s),))
        keep_layer(ni - 1, pl.ds(corner_row(s), SUB))

    def shape_rows(rows):
        for r in rows:
            row_at = me * nj + iota((SUB, LANES), 0) + (r - SUB)
            row_in = (row_at >= 0) & (row_at < groups * nj - 1)
            for t in range(every):
                col_at = my * nk + lane + (t * LANES if t < tiles else -LANES)
                cell = row_in & (col_at >= 0) & (col_at < slabs * nk - 1)

                @pl.loop(0, ni, unroll=4)
                def _(i, r=r, t=t, cell=cell):
                    for c in range(3):
                        sb[c, i, t, at(r), :] = sb[c, i, t, at(r), :] + warp[c, i, t, at(r), :]
                    keep = cell & (i < ni - 1)
                    sb[3, i, t, at(r), :] = jnp.where(keep, sb[3, i, t, at(r), :], 0.0)

    later = lax.rem(me, 2)
    sooner = 1 - later
    outer(sooner)
    for s in range(SWEEPS):
        sweep_a(s, s + 2, ni - 1, (outer_row(sooner),))

    unpack_lanes(shape_halos, ka_got, near_columns, 1, tile_rows)
    for message in surf:
        received(*message)
    for c in range(3):
        for r in range(0, all_rows, SUB):
            rows = slice(r, r + SUB)
            v0[c, 0, tiles, rows, :] = jnp.where(
                left_half, surf_got[0, c, rows, :], surf_got[1, c, rows, :]
            )
    keep_layer(0, slice(0, all_rows))
    for s in range(SWEEPS):
        sweep_a(s, 1, s + 2, tile_rows + [outer_row(sooner)])

    def cross(a, b):
        return (
            a[1] * b[2] - a[2] * b[1],
            a[2] * b[0] - a[0] * b[2],
            a[0] * b[1] - a[1] * b[0],
        )

    low_i[...] = jnp.zeros(low_i.shape, f32)
    arrived(load_cot)

    def gradients(parts):
        @pl.loop(0, ni, unroll=2)
        def _(i):
            above = jnp.minimum(i + 1, ni - 1)
            for r, full in parts:
                order = (tiles, *range(tiles)) if full else range(tiles)
                base = [[sb[c, i, t, at(r), :] for c in range(3)] for t in range(every)]
                held = None
                for t in order:
                    edge_i = [sb[c, above, t, at(r), :] - base[t][c] for c in range(3)]
                    edge_i[0] = edge_i[0] + 1.0
                    weight = sb[3, i, t, at(r), :]
                    weighted_i = [weight * e for e in edge_i]
                    if full:
                        edge_j = [sb[c, i, t, at(r + 1), :] - base[t][c] for c in range(3)]
                        edge_j[1] = edge_j[1] + 1.0
                        grad_k = cross(weighted_i, edge_j)
                    if t < tiles:
                        follow = base[(t + 1) % every]
                        edge_k = [
                            pltpu.roll(
                                jnp.where(first_lane, follow[c], base[t][c]), LANES - 1, 1
                            )
                            - base[t][c]
                            for c in range(3)
                        ]
                        edge_k[2] = edge_k[2] + 1.0
                        grad_j = cross(edge_k, weighted_i)
                        for c in range(3):
                            low_j[c, t, at(r), :] = grad_j[c]
                    if full and t < tiles:
                        grad_i = cross([weight * e for e in edge_j], edge_k)
                        rate = jnp.where((i > 0) & (i < ni - 1), inv[i, t, at(r), :], 0.0)
                        for c in range(3):
                            lower_k = pltpu.roll(
                                jnp.where(last_lane, held[c], grad_k[c]), 1, 1
                            )
                            out = adj[c, i, t, at(r), :] - grad_i[c] + low_i[c, t, at(r), :]
                            out = out + (low_j[c, t, at(r - 1), :] - grad_j[c])
                            out = out + (lower_k - grad_k[c])
                            low_i[c, t, at(r), :] = grad_i[c]
                            adj[c, i, t, at(r), :] = out
                            v0[c, i, t, at(r), :] = rate * out
                    if full:
                        held = grad_k

    flux_layers = [(c, i) for c in range(3) for i in inner]

    def send_flux(s):
        pack_rows(field, jc_send, 0, SWEEPS, 1, ni - 1, 2, (s,))

        @pl.when(either(s, near[:2]))
        def _():
            side_copy(s, jc_send, jc_got, 3).start()

    for message in surf:
        sent(*message)
    count = len(tile_rows)
    shape_rows([low_row + (1 - sooner) * SUB + n * SUB for n in range(count)])
    gradients([((1 - sooner) * SUB + n * SUB, n > 0) for n in range(count)])
    send_flux(later)

    def flux_lanes(number, at_row, rows):
        at_row = pl.multiple_of(at_row, SUB)
        return [
            (
                2 + s,
                kc_send.at[s, :, pl.ds(at_row - SUB, rows), :],
                kc_got.at[s, :, pl.ds(at_row, rows), :],
                number,
            )
            for s in (0, 1)
        ]

    edges_c = [edge(v0, c, i) for c, i in flux_layers]
    early_at, late_at = SUB + (1 - sooner) * SUB, SUB + sooner * (nj - SUB)
    early_rows = [early_at + n * SUB for n in range(count - 1)]
    early_lanes = flux_lanes(3, early_at, nj - SUB)
    late_lanes = flux_lanes(4, late_at, SUB)
    pack_lanes(edges_c, kc_send, 0, SWEEPS, early_rows)
    for message in early_lanes:
        start(*message)

    outer(later)
    for s in range(SWEEPS):
        sweep_a(s, 1, ni - 1, (outer_row(later),))
    shape_rows([outer_row(later)])
    gradients([((1 - later) * (nj - SUB) + n * SUB, n > 0) for n in range(2)])
    send_flux(sooner)
    pack_lanes(edges_c, kc_send, 0, SWEEPS, [late_at])
    for message in late_lanes + lanes_c:
        start(*message)
    for s in range(SWEEPS):
        for c in range(3):
            for i in (0, ni - 1):
                level[s][c, i] = jnp.zeros(v0.shape[2:], f32)

    sub = iota((SUB, LANES), 0)

    def sweep_c(s, first, stop, rows, adds):
        src = level[s]
        last = s == SWEEPS - 1
        inside = [
            None if add else (r + sub >= SUB + SWEEPS) & (r + sub < SUB + nj - SWEEPS)
            for r, add in zip(rows, adds)
        ]

        @in_pairs(first, stop)
        def _(i):
            for c in range(3):
                for r, add, keep in zip(rows, adds, inside):
                    low, high = add or whole
                    x, change = changes(src, c, i, r, tiles if last else every)
                    for t, delta in enumerate(change):
                        if t < tiles:
                            to = at(r + low, high - low)
                            part = delta[low:high] if add else jnp.where(keep, delta, 0.0)
                            adj[c, i, t, to, :] = adj[c, i, t, to, :] + part
                        if not last:
                            level[s + 1][c, i, t, at(r), :] = (
                                x[t] + inv[i, t, at(r), :] * delta
                            )

    whole = (0, SUB)
    flux_halos = [halo(v0, c, i) for c, i in flux_layers]
    for message in early_lanes:
        received(*message)
    unpack_lanes(flux_halos, kc_got, 0, SWEEPS, early_rows)
    inner_adds = [whole] * count
    inner_adds[0] = (SWEEPS, SUB)
    inner_adds[-1] = (0, SUB - SWEEPS)
    from_side = lambda n, side: [SUB + side * (nj - n * SUB) + k * SUB for k in range(n)]
    half = count // 2
    sweep_c(0, 1, ni - 1, from_side(half, later), [None] * half)
    sweep_c(1, 1, ni - 1, from_side(half - 1, later), [None] * (half - 1))
    for message in late_lanes:
        received(*message)
    unpack_lanes(flux_halos, kc_got, 0, SWEEPS, [late_at])
    sweep_c(0, 1, ni - 1, from_side(count - half, sooner), [None] * (count - half))
    rest = count - half + 1
    sweep_c(1, 1, ni - 1, from_side(rest, sooner), [None] * rest)
    for s in range(2, SWEEPS - 1):
        sweep_c(s, 1, ni - 1, tile_rows, inner_adds)
    mid_rows = shifted_rows[1:-1]
    sweep_c(SWEEPS - 1, 1, ni - 1, mid_rows, [whole] * len(mid_rows))

    for message in rows_c + lanes_c:
        received(*message)
    unpack_rows(field, jc_got, 0, SWEEPS, 1, ni - 1, 2)
    unpack_lanes(flux_halos, kc_got, 0, SWEEPS, (0, SUB + nj))
    for s in range(SWEEPS - 1):
        sweep_c(s, 1, SWEEPS - s, outer_rows, [whole] * 2)

    def add_wall(wall, layer):
        for c in range(3):
            for t in range(tiles):
                for r in tile_rows:
                    value = adj[c, wall, t, at(r), :]
                    for s in range(SWEEPS):
                        value = value + level[s][c, layer, t, at(r), :]
                    adj[c, wall, t, at(r), :] = value

    add_wall(0, 1)

    def wall_of(c):
        return jnp.concatenate([adj[c, 0, t, own, :] for t in range(tiles)], axis=1)

    wall = jnp.concatenate(
        [jnp.concatenate(split3(wall_of(c)), axis=0) for c in range(3)], axis=0
    )
    row_w = (me * nj + iota((nj, together * records), 0)).astype(f32)

    def reply_copy(step):
        to = lax.rem(me + step, groups)
        return pltpu.make_async_remote_copy(
            src_ref=reply_send.at[to],
            dst_ref=reply_got.at[me],
            send_sem=sem_reply.at[0, step],
            recv_sem=sem_reply.at[1, step],
            device_id=(to, my),
            device_id_type=MESH,
        )

    def answer(members):
        row, col = target_of(side_by_side([rec_got[g, 3:4, :] for g in members]))
        cols = (col_of == col).astype(bf16)
        here = row_w == row
        out = jnp.dot(wall, cols, preferred_element_type=f32)
        for c in range(3):
            first = 3 * c * nj
            value = (
                out[first : first + nj]
                + out[first + nj : first + 2 * nj]
                + out[first + 2 * nj : first + 3 * nj]
            )
            found = jnp.sum(jnp.where(here, value, 0.0), axis=0, keepdims=True)
            for n, g in enumerate(members):
                reply_send[g, c : c + 1, :] = found[:, n * records : (n + 1) * records]
        for g in members:
            reply_send[g, 3:4, :] = jnp.zeros((1, records), f32)

    def answer_next(n, last):
        steps = [n * together + k + 1 for k in range(together)]
        answer([lax.rem(me + step, groups) for step in steps])
        for step in steps[: together - 1] if last else steps:
            reply_copy(step).start()

    @pl.loop(0, groups // together - 1)
    def _(n):
        answer_next(n, False)

    answer_next(groups // together - 1, True)
    reply_got[me] = reply_send[me]

    for s in range(SWEEPS - 1):
        sweep_c(s, SWEEPS - s, ni - 1, outer_rows, [whole] * 2)
    sweep_c(SWEEPS - 1, 1, ni - 1, outer_rows, [whole] * 2)
    add_wall(ni - 1, ni - 2)

    for step in range(1, groups):
        reply_copy(step).wait_recv()
    total = lax.fori_loop(
        0, groups, lambda g, kept: kept + reply_got[g], jnp.zeros((4, records), f32)
    )
    weighted = jnp.concatenate(split3(total[0:3] * weights), axis=0)
    out = lax.dot_general(
        weighted, onehot_s, (((1,), (1,)), ((), ())), preferred_element_type=f32
    )
    sens_o[...] = out[0:3] + out[3:6] + out[6:9]
    for message in rows_a + lanes_a + rows_c + early_lanes + late_lanes + lanes_c:
        sent(*message)
    for step in range(1, groups):
        reply_copy(step).wait_send()
        rec_copy(step).wait_send()


def deliver(warp, adj, sens, warp_h, adj_h, sens_h, sem):
    nj, nk = warp_h.shape[2:]
    own = slice(SUB, SUB + nj)
    copies = []
    for n, (src, dst) in enumerate(((warp, warp_h), (adj, adj_h))):
        for c in range(3):
            for t in range(nk // LANES):
                lanes = slice(t * LANES, (t + 1) * LANES)
                copies.append(
                    pltpu.make_async_copy(
                        src.at[c, :, t, own, :], dst.at[c, :, :, lanes], sem.at[n, c, t]
                    )
                )
                copies[-1].start()
    sens_h[...] = sens[...]
    for copy in copies:
        copy.wait()


def body(
    struct_disp,
    rec_struct,
    rec_block,
    rec_node,
    rec_weight,
    offset,
    prior_warp,
    inv_volume,
    coord_cot,
    vol_cot,
):
    groups = lax.axis_size("blocks")
    slabs = lax.axis_size("span")
    _, ni, nj, nk = offset.shape
    records = rec_struct.shape[0]
    f32 = jnp.float32
    all_rows = nj + 2 * SUB
    tiles = nk // LANES
    _, _, total_rows = rows_plan(ni)
    cols_a = columns(3 * (ni - 1) + ni - 2, WIDE) + columns(4 * ni, 1)
    cols_c = columns(3 * (ni - 2), SWEEPS)
    rows_c = -(-3 * (ni - 2) * SWEEPS // SUB) * SUB

    def lane_buffers(count):
        return [
            pltpu.VMEM((2, count, nj, LANES), f32),
            pltpu.VMEM((2, count, all_rows, LANES), f32),
        ]

    vmem = pl.BlockSpec(memory_space=pltpu.VMEM)
    hbm = pl.BlockSpec(memory_space=pltpu.HBM)
    in_place = lambda x: pltpu.with_memory_space_constraint(x, pltpu.HBM)
    warp, adj, sens = pl.pallas_call(
        functools.partial(kernel, groups, slabs),
        out_shape=(
            pltpu.VMEM((3, ni, tiles + 1, all_rows, LANES), f32),
            pltpu.VMEM((3, ni, tiles, all_rows, LANES), f32),
            pltpu.VMEM(struct_disp.shape, f32),
        ),
        in_specs=[hbm] * 10,
        out_specs=[vmem] * 3,
        scratch_shapes=[
            *([pltpu.VMEM((3, ni, tiles + 1, all_rows, LANES), f32)] * SWEEPS),
            pltpu.VMEM((ni, tiles + 1, all_rows, LANES), f32),
            pltpu.VMEM((4, ni, tiles + 1, all_rows, LANES), f32),
            pltpu.VMEM((3, tiles, nj + SUB, LANES), f32),
            pltpu.VMEM((3, tiles, nj + SUB, LANES), f32),
            pltpu.VMEM((4, records), f32),
            pltpu.VMEM((groups, 4, records), f32),
            pltpu.VMEM((groups, 4, records), f32),
            pltpu.VMEM((groups, 4, records), f32),
            *([pltpu.VMEM((2, tiles, total_rows, LANES), f32)] * 2),
            *lane_buffers(cols_a),
            pltpu.VMEM((2, 3, all_rows, LANES), f32),
            *([pltpu.VMEM((2, tiles, rows_c, LANES), f32)] * 2),
            *lane_buffers(cols_c),
            *([pltpu.VMEM((records,), jnp.int32)] * 3),
            pltpu.VMEM((records,), f32),
            pltpu.VMEM(struct_disp.shape, f32),
            pltpu.SemaphoreType.DMA((5,)),
            pltpu.SemaphoreType.DMA((2, groups)),
            pltpu.SemaphoreType.DMA((2, groups)),
            pltpu.SemaphoreType.DMA((2, 5, 8)),
            pltpu.SemaphoreType.DMA((5, tiles)),
        ],
        compiler_params=pltpu.CompilerParams(
            collective_id=0, has_side_effects=True, vmem_limit_bytes=VMEM_LIMIT
        ),
        name="warp_adjoint",
    )(
        *map(
            in_place,
            (
                rec_struct,
                rec_block.reshape(records),
                rec_node,
                rec_weight,
                struct_disp,
                offset,
                prior_warp,
                inv_volume,
                coord_cot,
                vol_cot,
            ),
        )
    )
    return pl.pallas_call(
        deliver,
        out_shape=(
            jax.ShapeDtypeStruct(offset.shape, f32),
            jax.ShapeDtypeStruct(offset.shape, f32),
            jax.ShapeDtypeStruct(struct_disp.shape, f32),
        ),
        in_specs=[vmem] * 3,
        out_specs=[hbm, hbm, vmem],
        scratch_shapes=[pltpu.SemaphoreType.DMA((2, 3, tiles))],
        compiler_params=pltpu.CompilerParams(vmem_limit_bytes=4 * 1024 * 1024),
        name="deliver",
    )(warp, adj, sens)


def solution(mesh):
    placed = (
        P(None, ("blocks", "span")),
        P(("blocks", "span")),
        P(("blocks", "span"), None),
        P(("blocks", "span")),
        P(("blocks", "span")),
        P(None, None, "blocks", "span"),
        P(None, None, "blocks", "span"),
        P(None, "blocks", "span"),
        P(None, None, "blocks", "span"),
        P(None, "blocks", "span"),
    )
    return jax.shard_map(
        body,
        mesh=mesh,
        in_specs=placed,
        out_specs=(
            P(None, None, "blocks", "span"),
            P(None, None, "blocks", "span"),
            P(None, ("blocks", "span")),
        ),
        check_vma=False,
    )
```
